32 devices in a mesh: expert: 16 (over z, x, core), shard: 2 (over y).
Axes of the slice: x: 2, y: 2, z: 4, core: 2. Of those that a mesh axis runs over, the one named last changes fastest.
Arguments:
- tokens: bfloat16 [4096, 2048], P(('expert', 'shard')), may hold values from -6 to 6
- segment_ids: int32 [32, 128], P(('expert', 'shard')), may hold values from 0 to 3, never falling along the last dimension, each value on 1 to 64 neighbouring positions
- routes: int32 [4096, 6], P(('expert', 'shard')), may hold values from 0 to 15, all different within a row; in each aligned block of 128 rows (0 to 127, 128 to 255, ...) at most 96 rows name the same one
- attn_gain: bfloat16 [2048], P('shard'), may hold values from 0.5 to 1.5
- w_query: bfloat16 [2048, 3072], P('shard'), may hold values from -0.125 to 0.125
- w_latent: bfloat16 [2048, 576], P('shard'), may hold values from -0.125 to 0.125
- latent_gain: bfloat16 [512], P('shard'), may hold values from 0.5 to 1.5
- w_keyval: bfloat16 [512, 4096], P('shard'), may hold values from -0.25 to 0.25
- w_output: bfloat16 [2048, 2048], P('shard'), may hold values from -0.5 to 0.5
- ffn_gain: bfloat16 [2048], P('shard'), may hold values from 0.5 to 1.5
- w_router: bfloat16 [2048, 16], P('shard'), may hold values from -0.125 to 0.125
- shared_gate: bfloat16 [2048, 1408], P('shard'), may hold values from -0.125 to 0.125
- shared_up: bfloat16 [2048, 1408], P('shard'), may hold values from -0.125 to 0.125
- shared_down: bfloat16 [1408, 2048], P('shard'), may hold values from -0.15625 to 0.15625
- expert_gate: bfloat16 [16, 2048, 1408], P('expert', None, 'shard'), may hold values from -0.125 to 0.125
- expert_up: bfloat16 [16, 2048, 1408], P('expert', None, 'shard'), may hold values from -0.125 to 0.125
- expert_down: bfloat16 [16, 1408, 2048], P('expert', 'shard'), may hold values from -0.15625 to 0.15625
- cotangent: bfloat16 [4096, 2048], P(('expert', 'shard')), may hold values from -6 to 6
Outputs:
- block_out: bfloat16 [4096, 2048], P(('expert', 'shard'))
- tokens_grad: float32 [4096, 2048], P(('expert', 'shard'))
- attn_gain_grad: float32 [2048], P('shard')
- w_query_grad: float32 [2048, 3072], P('shard')
- w_latent_grad: float32 [2048, 576], P('shard')
- latent_gain_grad: float32 [512], P('shard')
- w_keyval_grad: float32 [512, 4096], P('shard')
- w_output_grad: float32 [2048, 2048], P('shard')
- ffn_gain_grad: float32 [2048], P('shard')
- w_router_grad: float32 [2048, 16], P('shard')
- shared_gate_grad: float32 [2048, 1408], P('shard')
- shared_up_grad: float32 [2048, 1408], P('shard')
- shared_down_grad: float32 [1408, 2048], P('shard')
- expert_gate_grad: float32 [16, 2048, 1408], P('expert', None, 'shard')
- expert_up_grad: float32 [16, 2048, 1408], P('expert', None, 'shard')
- expert_down_grad: float32 [16, 1408, 2048], P('expert', 'shard')
The draws below stay inside these ranges and needn't reach their ends.
Inputs may be any that keep to these rules, and one draw needn't show every extreme that they name: `segment_ids`: within each row the document numbers never fall; a document holds 1 to 64 tokens, and some document holds exactly 64. `routes`: A token's 6 experts differ; among the 128 tokens of one device no expert is named more than 96 times, and in some device some expert is named exactly 96 times.
All inputs are finite; a program needn't handle non-finite values.
Results may differ from the reference program's by a relative error of at most 0.019.
Values may be sent and summed in bfloat16 or wider, within the bound.
No kernel may reach another device: no remote copies, remote signals or barrier semaphores. Data moves between devices by JAX's collectives and lax.ppermute only.
A program may use at most 512 MiB of HBM per device.

```python
import math
import jax
import jax.numpy as jnp
import numpy as np
from jax import lax

D = 2048
HEADS = 16
NOPE = 128
ROPE = 64
VDIM = 128
KVR = 512
MFF = 1408
SFF = 1408
TOP = 6
SEGS = 4
TOK_DEV = 128
SEQ_MOST = 64
EXPERTS = 16
CAP = 96
TOKENS = 4096
N_EXPERT = 16
N_SHARD = 2


def block_levels(stream_key, shape, cuts, least, largest):
    def one(dim, shards_of):
        steps = jax.random.uniform(jax.random.fold_in(jax.random.fold_in(stream_key, 6), dim), (shards_of,), jnp.float32, least / len(cuts), largest / len(cuts))
        return jnp.repeat(jnp.exp(steps), shape[dim] // shards_of).reshape((-1,) + (1,) * (len(shape) - dim - 1))

    loudness = one(*cuts[0])
    for cut in cuts[1:]:
        loudness = loudness * one(*cut)
    return loudness


def split_up(number_of, total, bound, slope):
    portions = [(1 << 20) // math.isqrt(rank ** slope) + 1 for rank in range(2, number_of + 1)]
    rest, given = total - bound - (number_of - 1), [1] * (number_of - 1)
    while rest > 0:
        candidates = [i for i in range(number_of - 1) if given[i] < bound]
        whole, left = sum([portions[i] for i in candidates]), rest
        for i in candidates:
            extra = min(bound - given[i], max(1, left * portions[i] // whole), rest)
            given[i] = given[i] + extra
            rest = rest - extra
    return np.array([bound] + given)


def uneven(rng, count, total, limit, skew):
    if count == 2:
        one = jax.random.randint(rng, (), max(1, total - limit), min(limit, total - 1) + 1)
        return jnp.stack([one, total - one])
    sizes = jnp.asarray(split_up(count, total, limit, skew), jnp.int32)
    twos = (count - 1) // 2
    source_of, taker = sizes[1:1 + 2 * twos:2], sizes[2:2 + 2 * twos:2]
    room = jnp.minimum(source_of - 1, limit - taker)
    shifted = jax.random.randint(jax.random.fold_in(rng, 1), (twos,), 0, 1 << 20) % (room + 1)
    sizes = sizes.at[1:1 + 2 * twos:2].set(source_of - shifted).at[2:2 + 2 * twos:2].set(taker + shifted)
    return sizes[jax.random.permutation(jax.random.fold_in(rng, 2), count)]


def deal_out(rng, own, number, rows, number_of, top, reach, lean):
    sequence = jax.random.permutation(rng, number_of)
    packed, common = shares(number_of, rows * top, reach, lean, True), shares(number_of, rows * top, reach, lean, False)
    places = jnp.arange(number_of)

    def named(lengths, rotation):
        used = int((lengths > 0).sum())
        fixed = max(1, used // 4)
        passed = fixed + (places - fixed + rotation * (used - fixed)) % max(1, number_of - fixed)
        return jnp.zeros((number_of,), jnp.int32).at[sequence[jnp.where(places < fixed, places, passed)]].set(jnp.asarray(lengths, jnp.int32))

    lengths = jnp.where(number % 4 == 0, named(packed, number // 4), named(common, number - number // 4 - 1))
    mixed = jax.random.permutation(jax.random.fold_in(own, 3), number_of)
    donor, sink = mixed[0:number_of // 2 * 2:2], mixed[1:number_of // 2 * 2:2]
    room = jnp.minimum(lengths[donor] - 1, reach - lengths[sink]) // 2
    room = jnp.where((donor == sequence[0]) | (sink == sequence[0]) | (lengths[sink] == 0), 0, jnp.maximum(room, 0))
    passed = jax.random.randint(jax.random.fold_in(own, 4), (number_of // 2,), 0, 1 << 20) % (room + 1)
    lengths = lengths.at[donor].add(-passed).at[sink].add(passed)
    labels = jnp.searchsorted(jnp.cumsum(lengths), jnp.arange(rows * top), side="right").astype(jnp.int32)
    listing = labels.reshape(top, rows).T
    listing = listing[jax.random.permutation(jax.random.fold_in(own, 1), rows)]
    rotation = jax.random.randint(jax.random.fold_in(own, 2), (rows, 1), 0, top)
    return jnp.take_along_axis(listing, (jnp.arange(top)[None, :] + rotation) % top, axis=1)


def shares(count, total, bound, skew, full):
    loads = [(1 << 20) // math.isqrt(rank ** skew) + 1 for rank in range(1, count + 1)]
    largest = bound if full else min(bound, max(-(-total // count), total * loads[0] // sum(loads)))
    least = 1 if total - largest >= count - 1 else 0
    counts, spare = [largest] + [least] * (count - 1), total - largest - least * (count - 1)
    while spare > 0:
        movable = [i for i in range(1, count) if counts[i] < largest] or [i for i in range(1, count) if counts[i] < bound]
        whole, left = sum([loads[i] for i in movable]), spare
        for i in movable:
            addition = min(bound - counts[i], max(1, left * loads[i] // whole), spare)
            counts[i] = counts[i] + addition
            spare = spare - addition
    return np.array(counts)


def bell_draw(own_key, shape, deviation, bound, cuts=(), held_as=jnp.bfloat16):
    result = deviation * jax.random.normal(own_key, shape, jnp.float32)
    if cuts:
        result = result * block_levels(own_key, shape, cuts, -0.22, 0.18)
    return jnp.clip(result, -bound, bound).astype(held_as)


def setup_inputs(seed: int = 0) -> dict:
    keys = jax.random.split(jax.random.key(seed), 19)
    tokens = bell_draw(keys[0], (TOKENS, D), 1.0, 6.0, ((0, 32),))
    segment_ids = jax.vmap(lambda own: jnp.searchsorted(jnp.cumsum(uneven(own, SEGS, TOK_DEV, SEQ_MOST, 2)), jnp.arange(TOK_DEV), side="right"))(jax.random.split(keys[1], (N_EXPERT * N_SHARD))).reshape((N_EXPERT * N_SHARD, TOK_DEV)).astype(jnp.int32)
    routes_keys = jax.random.split(jax.random.fold_in(keys[2], 1), TOKENS // TOK_DEV)
    routes_turns = jax.random.permutation(jax.random.fold_in(keys[2], 3), TOKENS // TOK_DEV)
    routes = jax.vmap(lambda own, number: deal_out(jax.random.fold_in(keys[2], 2), own, number, TOK_DEV, EXPERTS, TOP, CAP, 2))(routes_keys, routes_turns).reshape((TOKENS, TOP))
    attn_gain = jnp.clip(1.0 + 0.1 * jax.random.normal(keys[3], (D,), jnp.float32), 0.5, 1.5).astype(jnp.bfloat16)
    w_query = bell_draw(keys[4], (D, HEADS * (NOPE + ROPE)), D ** -0.5, 0.125, ((0, 2),))
    w_latent = bell_draw(keys[5], (D, KVR + ROPE), D ** -0.5, 0.125, ((0, 2),))
    latent_gain = jnp.clip(1.0 + 0.1 * jax.random.normal(keys[6], (KVR,), jnp.float32), 0.5, 1.5).astype(jnp.bfloat16)
    w_keyval = bell_draw(keys[7], (KVR, HEADS * (NOPE + VDIM)), KVR ** -0.5, 0.25, ((0, 2),))
    w_output = bell_draw(keys[8], (HEADS * VDIM, D), (HEADS * VDIM // 16) ** -0.5, 0.5, ((0, 2),))
    ffn_gain = jnp.clip(1.0 + 0.1 * jax.random.normal(keys[9], (D,), jnp.float32), 0.5, 1.5).astype(jnp.bfloat16)
    w_router = bell_draw(keys[10], (D, EXPERTS), D ** -0.5, 0.125, ((0, 2),))
    shared_gate = bell_draw(keys[11], (D, SFF), D ** -0.5, 0.125, ((0, 2),))
    shared_up = bell_draw(keys[12], (D, SFF), D ** -0.5, 0.125, ((0, 2),))
    shared_down = bell_draw(keys[13], (SFF, D), SFF ** -0.5, 0.15625, ((0, 2),))
    expert_gate = bell_draw(keys[14], (EXPERTS, D, MFF), D ** -0.5, 0.125, ((0, 16), (2, 2)))
    expert_up = bell_draw(keys[15], (EXPERTS, D, MFF), D ** -0.5, 0.125, ((0, 16), (2, 2)))
    expert_down = bell_draw(keys[16], (EXPERTS, MFF, D), MFF ** -0.5, 0.15625, ((0, 16), (1, 2)))
    cotangent = bell_draw(keys[17], (TOKENS, D), 1.0, 6.0, ((0, 32),))
    return {"tokens": tokens, "segment_ids": segment_ids, "routes": routes, "attn_gain": attn_gain, "w_query": w_query, "w_latent": w_latent, "latent_gain": latent_gain, "w_keyval": w_keyval, "w_output": w_output, "ffn_gain": ffn_gain, "w_router": w_router, "shared_gate": shared_gate, "shared_up": shared_up, "shared_down": shared_down, "expert_gate": expert_gate, "expert_up": expert_up, "expert_down": expert_down, "cotangent": cotangent}


NORM_EPSILON = 1e-06
ROTARY_BASE = 50000.0
ROUTE_SCALE = 2.446
NEGATIVE = -1e+30

def norm_scale(values):
    return lax.rsqrt(lax.optimization_barrier(jnp.mean(values * values, axis=-1, keepdims=True)) + NORM_EPSILON)

def norm_backward(upstream, values, scale_row, gain_row):
    normed = values * scale_row
    gain_grad = lax.optimization_barrier(jnp.sum(upstream * normed, axis=0))
    inner_grad = upstream * gain_row
    values_grad = scale_row * (inner_grad - normed * lax.optimization_barrier(jnp.mean(inner_grad * normed, axis=-1, keepdims=True)))
    return (values_grad, gain_grad)

def lead_product(former, latter):
    return jnp.dot(former.T, latter, preferred_element_type=jnp.float32)

def trail_product(former, latter):
    return jnp.dot(former, latter.T, preferred_element_type=jnp.float32)

def plain_product(former, latter):
    return jnp.dot(former, latter, preferred_element_type=jnp.float32)

def batched(pattern, former, latter):
    return jnp.einsum(pattern, former.astype(jnp.float32), latter.astype(jnp.float32))

def rotary_tables(segment_row):
    length = segment_row.shape[0]
    places = jnp.arange(length, dtype=jnp.int32)
    same_document = segment_row[:, None] == segment_row[None, :]
    position = lax.optimization_barrier(jnp.sum(jnp.where(same_document & (places[None, :] < places[:, None]), 1.0, 0.0), axis=1))
    half_rope = ROPE // 2
    frequency = ROTARY_BASE ** (-2.0 * jnp.arange(half_rope, dtype=jnp.float32) / ROPE)
    angles = position[:, None] * frequency[None, :]
    cosine = jnp.concatenate([jnp.cos(angles), jnp.cos(angles)], axis=1)
    sine_table = jnp.concatenate([jnp.sin(angles), jnp.sin(angles)], axis=1)
    allowed = same_document & (places[None, :] <= places[:, None])
    return (cosine, sine_table, allowed)

def rotate(values, cosine, sine_table):
    half_rope = values.shape[-1] // 2
    turned = jnp.concatenate([-values[..., half_rope:], values[..., :half_rope]], axis=-1)
    return values * cosine + turned * sine_table

def unrotate(upstream, cosine, sine_table):
    half_rope = upstream.shape[-1] // 2
    weighted = upstream * sine_table
    turned = jnp.concatenate([weighted[..., half_rope:], -weighted[..., :half_rope]], axis=-1)
    return upstream * cosine + turned

def attention_scores(query_b, key_b, allowed):
    scores = batched('thd,shd->hts', query_b, key_b) * (NOPE + ROPE) ** (-0.5)
    return jnp.where(allowed[None, :, :], scores, NEGATIVE)

def attend_forward(inputs, segment_row, weights):
    attn_gain, w_query, w_latent, latent_gain, w_keyval, w_output = weights
    row_count = inputs.shape[0]
    cosine, sine_table, allowed = rotary_tables(segment_row)
    scale_one = norm_scale(inputs)
    normed_one = (inputs * scale_one * attn_gain.astype(jnp.float32)).astype(jnp.bfloat16)
    queries = plain_product(normed_one, w_query).reshape(row_count, HEADS, NOPE + ROPE)
    query_turn = rotate(queries[:, :, NOPE:], cosine[:, None, :], sine_table[:, None, :])
    query_b = jnp.concatenate([queries[:, :, :NOPE], query_turn], axis=-1).astype(jnp.bfloat16)
    latent_all = plain_product(normed_one, w_latent)
    latent = latent_all[:, :KVR]
    key_rope = rotate(latent_all[:, KVR:], cosine, sine_table)
    scale_latent = norm_scale(latent)
    latent_normed = (latent * scale_latent * latent_gain.astype(jnp.float32)).astype(jnp.bfloat16)
    keyval = plain_product(latent_normed, w_keyval).reshape(row_count, HEADS, NOPE + VDIM)
    key_shared = jnp.broadcast_to(key_rope[:, None, :], (row_count, HEADS, ROPE))
    key_b = jnp.concatenate([keyval[:, :, :NOPE], key_shared], axis=-1).astype(jnp.bfloat16)
    value_b = keyval[:, :, NOPE:].astype(jnp.bfloat16)
    scores = attention_scores(query_b, key_b, allowed)
    peak_score = lax.optimization_barrier(jnp.max(scores, axis=-1, keepdims=True))
    raised = jnp.exp(scores - peak_score)
    totals = lax.optimization_barrier(jnp.sum(raised, axis=-1, keepdims=True))
    probs_b = (raised / totals).astype(jnp.bfloat16)
    log_total = peak_score + jnp.log(totals)
    attended = batched('hts,shd->thd', probs_b, value_b).astype(jnp.bfloat16).reshape(row_count, HEADS * VDIM)
    residual = inputs + plain_product(attended, w_output)
    return {'inputs': inputs, 'scale_one': scale_one, 'normed_one': normed_one, 'latent': latent, 'scale_latent': scale_latent, 'latent_normed': latent_normed, 'query_b': query_b, 'key_b': key_b, 'value_b': value_b, 'log_total': log_total, 'attended': attended, 'cosine': cosine, 'sine_table': sine_table, 'allowed': allowed, 'residual': residual}

def attend_backward(residual_grad, saved, weights):
    attn_gain, w_query, w_latent, latent_gain, w_keyval, w_output = weights
    row_count = residual_grad.shape[0]
    grad_b = residual_grad.astype(jnp.bfloat16)
    output_grad = lead_product(saved['attended'], grad_b)
    attended_grad = trail_product(grad_b, w_output).astype(jnp.bfloat16).reshape(row_count, HEADS, VDIM)
    scores = attention_scores(saved['query_b'], saved['key_b'], saved['allowed'])
    probabilities = jnp.exp(scores - saved['log_total'])
    value_grad = batched('hts,thd->shd', probabilities.astype(jnp.bfloat16), attended_grad)
    probs_grad = batched('thd,shd->hts', attended_grad, saved['value_b'])
    center = lax.optimization_barrier(jnp.sum(probabilities * probs_grad, axis=-1, keepdims=True))
    scores_grad = (probabilities * (probs_grad - center) * (NOPE + ROPE) ** (-0.5)).astype(jnp.bfloat16)
    query_grad = batched('hts,shd->thd', scores_grad, saved['key_b'])
    key_grad = batched('hts,thd->shd', scores_grad, saved['query_b'])
    cosine = saved['cosine']
    sine_table = saved['sine_table']
    query_turn_grad = unrotate(query_grad[:, :, NOPE:], cosine[:, None, :], sine_table[:, None, :])
    query_grad_b = jnp.concatenate([query_grad[:, :, :NOPE], query_turn_grad], axis=-1).astype(jnp.bfloat16).reshape(row_count, HEADS * (NOPE + ROPE))
    query_w_grad = lead_product(saved['normed_one'], query_grad_b)
    normed_grad = trail_product(query_grad_b, w_query)
    key_rope_grad = unrotate(lax.optimization_barrier(jnp.sum(key_grad[:, :, NOPE:], axis=1)), cosine, sine_table)
    keyval_grad_b = jnp.concatenate([key_grad[:, :, :NOPE], value_grad], axis=-1).astype(jnp.bfloat16).reshape(row_count, HEADS * (NOPE + VDIM))
    keyval_w_grad = lead_product(saved['latent_normed'], keyval_grad_b)
    latent_normed_grad = trail_product(keyval_grad_b, w_keyval)
    latent_grad, latent_gain_grad = norm_backward(latent_normed_grad, saved['latent'], saved['scale_latent'], latent_gain.astype(jnp.float32))
    latent_all_grad = jnp.concatenate([latent_grad, key_rope_grad], axis=-1).astype(jnp.bfloat16)
    latent_w_grad = lead_product(saved['normed_one'], latent_all_grad)
    normed_grad = normed_grad + trail_product(latent_all_grad, w_latent)
    inputs_grad, attn_gain_grad = norm_backward(normed_grad, saved['inputs'], saved['scale_one'], attn_gain.astype(jnp.float32))
    return (residual_grad + inputs_grad, (attn_gain_grad, query_w_grad, latent_w_grad, latent_gain_grad, keyval_w_grad, output_grad))

def route_gates(normed_two, route_rows, w_router):
    expert_total = w_router.shape[1]
    scores = jax.nn.sigmoid(plain_product(normed_two, w_router))
    chosen_mask = route_rows[:, :, None] == jnp.arange(expert_total, dtype=jnp.int32)[None, None, :]
    picked = lax.optimization_barrier(jnp.sum(jnp.where(chosen_mask, scores[:, None, :], 0.0), axis=2))
    gate_values = ROUTE_SCALE * picked / lax.optimization_barrier(jnp.sum(picked, axis=1, keepdims=True))
    return (gate_values, picked, chosen_mask)

def reference(tokens, segment_ids, routes, attn_gain, w_query, w_latent, latent_gain, w_keyval, w_output, ffn_gain, w_router, shared_gate, shared_up, shared_down, expert_gate, expert_up, expert_down, cotangent):
    attn_weights = (attn_gain, w_query, w_latent, latent_gain, w_keyval, w_output)
    block_total = N_EXPERT * N_SHARD
    token_blocks = tokens.reshape(block_total, TOK_DEV, D)
    route_blocks = routes.reshape(block_total, TOK_DEV, TOP)
    cotangent_blocks = cotangent.reshape(block_total, TOK_DEV, D)

    def forward_block(carry, pieces):
        block_tokens, block_segments, block_routes = pieces
        saved = attend_forward(block_tokens.astype(jnp.float32), block_segments, attn_weights)
        residual = saved['residual']
        normed_two = (residual * norm_scale(residual) * ffn_gain.astype(jnp.float32)).astype(jnp.bfloat16)
        gate_values, picked, chosen_mask = route_gates(normed_two, block_routes, w_router)
        return (carry, (normed_two, gate_values))
    unused, (normed_blocks, gate_blocks) = lax.scan(forward_block, jnp.zeros((), jnp.float32), (token_blocks, segment_ids, route_blocks))
    row_total = TOKENS * TOP
    flat_routes = routes.reshape(-1)
    normed_padded = jnp.concatenate([normed_blocks.reshape(TOKENS, D), jnp.zeros((1, D), jnp.bfloat16)], axis=0)
    gate_padded = jnp.concatenate([gate_blocks.reshape(-1), jnp.zeros((1,), jnp.float32)], axis=0)
    upstream_padded = jnp.concatenate([cotangent.astype(jnp.float32), jnp.zeros((1, D), jnp.float32)], axis=0)
    quarter = MFF // N_SHARD

    def expert_step(carry, pieces):
        routed, normed_grad, gate_grads = carry
        gate_weight, up_weight, down_weight, expert_id = pieces
        chosen = jnp.nonzero(flat_routes == expert_id, size=N_EXPERT * N_SHARD * CAP, fill_value=row_total)[0].astype(jnp.int32)
        token_index = chosen // TOP
        expert_rows = normed_padded[token_index]
        pre_gate = plain_product(expert_rows, gate_weight)
        pre_up = plain_product(expert_rows, up_weight)
        sig_gate = jax.nn.sigmoid(pre_gate)
        hidden = (pre_gate * sig_gate * pre_up).astype(jnp.bfloat16)
        output_sum = jnp.zeros((expert_rows.shape[0], D), jnp.float32)
        for part_index in range(N_SHARD):
            lower = part_index * quarter
            term = plain_product(hidden[:, lower:lower + quarter], down_weight[lower:lower + quarter, :])
            output_sum = output_sum + lax.optimization_barrier(term.astype(jnp.bfloat16)).astype(jnp.float32)
        expert_out = output_sum.astype(jnp.bfloat16).astype(jnp.float32)
        gate_rows = gate_padded[chosen]
        upstream_rows = upstream_padded[token_index]
        routed = routed.at[token_index].add(gate_rows[:, None] * expert_out)
        gate_grads = gate_grads.at[chosen].set(lax.optimization_barrier(jnp.sum(upstream_rows * expert_out, axis=1)))
        grad_rows = (gate_rows[:, None] * upstream_rows).astype(jnp.bfloat16)
        down_grad = lead_product(hidden, grad_rows)
        hidden_grad = trail_product(grad_rows, down_weight)
        pre_gate_grad = (hidden_grad * pre_up * sig_gate * (1.0 + pre_gate * (1.0 - sig_gate))).astype(jnp.bfloat16)
        pre_up_grad = (hidden_grad * pre_gate * sig_gate).astype(jnp.bfloat16)
        gate_w_grad = lead_product(expert_rows, pre_gate_grad)
        up_w_grad = lead_product(expert_rows, pre_up_grad)
        input_sum = jnp.zeros((expert_rows.shape[0], D), jnp.float32)
        for part_index in range(N_SHARD):
            lower = part_index * quarter
            term = trail_product(pre_gate_grad[:, lower:lower + quarter], gate_weight[:, lower:lower + quarter])
            term = term + trail_product(pre_up_grad[:, lower:lower + quarter], up_weight[:, lower:lower + quarter])
            input_sum = input_sum + lax.optimization_barrier(term.astype(jnp.bfloat16)).astype(jnp.float32)
        input_rows = input_sum.astype(jnp.bfloat16).astype(jnp.float32)
        normed_grad = normed_grad.at[token_index].add(input_rows)
        return ((routed, normed_grad, gate_grads), (gate_w_grad, up_w_grad, down_grad))
    start_carry = (jnp.zeros((TOKENS + 1, D), jnp.float32), jnp.zeros((TOKENS + 1, D), jnp.float32), jnp.zeros((row_total + 1,), jnp.float32))
    expert_ids = jnp.arange(EXPERTS, dtype=jnp.int32)
    (routed_all, normed_grad_all, gate_grad_all), (expert_gate_grad, expert_up_grad, expert_down_grad) = lax.scan(expert_step, start_carry, (expert_gate, expert_up, expert_down, expert_ids))
    routed_blocks = routed_all[:TOKENS].reshape(block_total, TOK_DEV, D)
    normed_grad_blocks = normed_grad_all[:TOKENS].reshape(block_total, TOK_DEV, D)
    gate_grad_blocks = gate_grad_all[:row_total].reshape(block_total, TOK_DEV, TOP)
    mixer_weights = attn_weights + (ffn_gain, w_router, shared_gate, shared_up, shared_down)

    def backward_block(carry, pieces):
        block_tokens, block_segments, block_routes, block_cotangent, block_routed, block_normed_grad, block_gate_grads = pieces
        saved = attend_forward(block_tokens.astype(jnp.float32), block_segments, attn_weights)
        residual = saved['residual']
        scale_two = norm_scale(residual)
        normed_two = (residual * scale_two * ffn_gain.astype(jnp.float32)).astype(jnp.bfloat16)
        gate_values, picked, chosen_mask = route_gates(normed_two, block_routes, w_router)
        shared_pre_gate = plain_product(normed_two, shared_gate)
        shared_pre_up = plain_product(normed_two, shared_up)
        shared_sig = jax.nn.sigmoid(shared_pre_gate)
        shared_hidden = (shared_pre_gate * shared_sig * shared_pre_up).astype(jnp.bfloat16)
        block_out = (residual + block_routed + plain_product(shared_hidden, shared_down)).astype(jnp.bfloat16)
        upstream = block_cotangent.astype(jnp.float32)
        shared_down_grad = lead_product(shared_hidden, block_cotangent)
        shared_hidden_grad = trail_product(block_cotangent, shared_down)
        shared_gate_pre_grad = (shared_hidden_grad * shared_pre_up * shared_sig * (1.0 + shared_pre_gate * (1.0 - shared_sig))).astype(jnp.bfloat16)
        shared_up_pre_grad = (shared_hidden_grad * shared_pre_gate * shared_sig).astype(jnp.bfloat16)
        shared_gate_grad = lead_product(normed_two, shared_gate_pre_grad)
        shared_up_grad = lead_product(normed_two, shared_up_pre_grad)
        normed_two_grad = block_normed_grad + trail_product(shared_gate_pre_grad, shared_gate) + trail_product(shared_up_pre_grad, shared_up)
        picked_total = lax.optimization_barrier(jnp.sum(picked, axis=1, keepdims=True))
        weighted = lax.optimization_barrier(jnp.sum(block_gate_grads * picked, axis=1, keepdims=True))
        picked_grad = ROUTE_SCALE * (block_gate_grads / picked_total - weighted / (picked_total * picked_total))
        logit_pick = picked_grad * picked * (1.0 - picked)
        logit_grad_b = lax.optimization_barrier(jnp.sum(jnp.where(chosen_mask, logit_pick[:, :, None], 0.0), axis=1)).astype(jnp.bfloat16)
        router_grad = lead_product(normed_two, logit_grad_b)
        normed_two_grad = normed_two_grad + trail_product(logit_grad_b, w_router)
        residual_norm_grad, ffn_gain_grad = norm_backward(normed_two_grad, residual, scale_two, ffn_gain.astype(jnp.float32))
        residual_grad = upstream + residual_norm_grad
        tokens_grad, attn_grads = attend_backward(residual_grad, saved, attn_weights)
        block_grads = attn_grads + (ffn_gain_grad, router_grad, shared_gate_grad, shared_up_grad, shared_down_grad)
        return (jax.tree.map(jnp.add, carry, block_grads), (block_out, tokens_grad))
    zero_grads = tuple((jnp.zeros(weight.shape, jnp.float32) for weight in mixer_weights))
    mixer_grads, (out_blocks, grad_blocks) = lax.scan(backward_block, zero_grads, (token_blocks, segment_ids, route_blocks, cotangent_blocks, routed_blocks, normed_grad_blocks, gate_grad_blocks))
    return (out_blocks.reshape(TOKENS, D), grad_blocks.reshape(TOKENS, D), mixer_grads[0], mixer_grads[1], mixer_grads[2], mixer_grads[3], mixer_grads[4], mixer_grads[5], mixer_grads[6], mixer_grads[7], mixer_grads[8], mixer_grads[9], mixer_grads[10], expert_gate_grad, expert_up_grad, expert_down_grad)
```

```python
import functools

import jax
import jax.numpy as jnp
import numpy as np
from jax import lax
from jax.experimental import pallas as pl
from jax.experimental.pallas import tpu as pltpu
from jax.sharding import PartitionSpec as P

HEADS = 16
NOPE = 128
ROPE = 64
VDIM = 128
KVR = 512
NORM_EPSILON = 1e-06
ROTARY_BASE = 50000.0
ROUTE_SCALE = 2.446
NEGATIVE = -1e30
F32 = jnp.float32
BF16 = jnp.bfloat16


def dot(a, b):
    return jnp.dot(a, b, preferred_element_type=F32)


def dot_tl(a, b):
    return lax.dot_general(a, b, (((0,), (0,)), ((), ())), preferred_element_type=F32)


def dot_tr(a, b):
    return lax.dot_general(a, b, (((1,), (1,)), ((), ())), preferred_element_type=F32)


def norm_scale(values):
    return lax.rsqrt(jnp.mean(values * values, axis=-1, keepdims=True) + NORM_EPSILON)


def zero_of(*marks):
    total = jnp.zeros((), F32)
    for mark in jax.tree.leaves(marks):
        one = lax.slice(mark, (0,) * mark.ndim, (1,) * mark.ndim).reshape(())
        total = total + (one != one).astype(F32)
    return total


def after(value, *marks):
    zero = zero_of(*marks)
    return jax.tree.map(lambda v: v + zero.astype(v.dtype), value)


def add_b(a, b):
    return (a.astype(F32) + b.astype(F32)).astype(BF16)


class Net:
    def __init__(self):
        self.E = lax.axis_size("expert")
        self.S = lax.axis_size("shard")
        nx = self.S if self.E % (2 * self.S) == 0 else 1
        nc = 2 if self.E % 2 == 0 else 1
        self.n = {"c": nc, "x": nx, "z": self.E // (nc * nx), "y": self.S}
        self.stride = {"c": 1, "x": nc, "z": nc * nx}
        self.e = lax.axis_index("expert")
        self.s = lax.axis_index("shard")

    def pos(self, axis):
        if axis == "y":
            return self.s
        return (self.e // self.stride[axis]) % self.n[axis]

    def hop(self, value, axis, k=1):
        n = self.n[axis]
        if axis == "y":
            return lax.ppermute(value, "shard", [(i, (i + k) % n) for i in range(n)])
        st = self.stride[axis]
        pairs = []
        for i in range(self.E):
            p = (i // st) % n
            pairs.append((i, i + ((p + k) % n - p) * st))
        return lax.ppermute(value, "expert", pairs)

    def ring_gather(self, value, axis):
        n = self.n[axis]
        out = [None] * n
        out[0] = value
        cur = value
        for k in range(1, n):
            cur = self.hop(cur, axis)
            out[n - k] = cur
        return out

    def ring_scatter(self, value, axis, dim, add):
        n = self.n[axis]
        take = lambda r: lax.index_in_dim(value, r, dim, keepdims=False)
        acc = take(n - 1)
        for k in range(1, n):
            acc = add(take(n - 1 - k), self.hop(acc, axis))
        return acc

    def absolute(self, pieces, axis, dim):
        n = self.n[axis]
        i = self.pos(axis)
        if n == 1:
            return pieces[0]
        if n == 2:
            first = jnp.concatenate(pieces, axis=dim)
            second = jnp.concatenate(pieces[::-1], axis=dim)
            return jnp.where(i == 0, first, second)
        size = pieces[0].shape[dim]
        twice = jnp.concatenate(list(pieces) * 2, axis=dim)
        return lax.dynamic_slice_in_dim(twice, ((n - i) % n) * size, n * size, dim)

    def gather_part(self, value, mid, mark):
        last = "y" if mid == "x" else "x"
        cur = jnp.stack(self.ring_gather(value, "z"), axis=0)
        pieces = self.ring_gather(cur, mid)
        cur = jnp.stack(pieces[:1] + after(pieces[1:], mark), axis=0)
        return self.ring_gather(cur, "c"), self.ring_gather(cur, last)[1:]

    def scatter_cores(self, bufs):
        return [self.ring_list(pieces, "c") for pieces in bufs]

    def scatter_stage(self, lists, axes, work=None):
        n = max(self.n[axis] for axis in axes)
        accs = [pieces[self.n[axis] - 1] for pieces, axis in zip(lists, axes)]
        for k in range(1, n):
            got = [
                self.hop(acc, axis) if k < self.n[axis] else None for acc, axis in zip(accs, axes)
            ]
            job = None
            if work:
                job = work.pop(0)
            if job is not None:
                mark = job(accs)
                got = [g if g is None else after(g, mark) for g in got]
            accs = [
                acc if g is None else add_b(pieces[self.n[axis] - 1 - k], g)
                for acc, g, pieces, axis in zip(accs, got, lists, axes)
            ]
        return accs

    def scatter_both(self, sums_1, sums_2, work=None):
        work = list(work or [])
        split = lambda v: [v[k] for k in range(v.shape[0])]
        one, two = self.scatter_stage([sums_1, sums_2], ("y", "x"), work)
        one, two = self.scatter_stage([split(one), split(two)], ("x", "y"), work)
        rows = [jnp.concatenate([one[k], two[k]], axis=0) for k in range(self.n["z"])]
        return self.scatter_stage([rows], ("z",), work)[0]

    def ring_list(self, pieces, axis):
        n = self.n[axis]
        acc = pieces[n - 1]
        for k in range(1, n):
            acc = add_b(pieces[n - 1 - k], self.hop(acc, axis))
        return acc

    def reduce_steps(self, value, order):
        for axis in order:
            n, i = self.n[axis], self.pos(axis)
            if n == 1:
                continue
            rows = value.shape[0] // n
            take = lambda k, v=value: lax.dynamic_slice_in_dim(v, (k % n) * rows, rows, 0)
            got = yield [(take(i + k), axis, k) for k in range(1, n)]
            total = take(i).astype(F32)
            for piece in got:
                total = total + piece.astype(F32)
            value = total.astype(BF16)
        return value

    def spread_steps(self, value, order, dim=0):
        for axis in order[::-1]:
            n = self.n[axis]
            if n == 1:
                continue
            got = yield [(value, axis, k) for k in range(1, n)]
            value = self.absolute([value] + list(got)[::-1], axis, dim)
        return value

    def total_steps(self, value, order):
        value = yield from self.reduce_steps(value, order)
        value = yield from self.spread_steps(value, order)
        return value

    def in_rounds(self, runs):
        results = [None] * len(runs)
        sends = {k: next(run) for k, run in enumerate(runs)}
        while sends:
            keys = [k for k in sends if sends[k]]
            values = [[v[0] for v in sends[k]] for k in keys]
            got = {
                k: [self.hop(v, item[1], item[2]) for v, item in zip(vs, sends[k])]
                for k, vs in zip(keys, values)
            }
            following = {}
            for k in sends:
                try:
                    following[k] = runs[k].send(got.get(k))
                except StopIteration as stop:
                    results[k] = stop.value
            sends = following
        return results


MEGA = 2**20
LANES = 128


def dot_nt(a, b):
    return lax.dot_general(a, b, (((1,), (1,)), ((), ())), preferred_element_type=F32)


def fill_back(entries):
    out = list(entries)
    for i in reversed(range(len(out) - 1)):
        if out[i] is None:
            out[i] = out[i + 1]
    last = None
    for i in range(len(out)):
        last = out[i] if out[i] is not None else last
        out[i] = last
    return out


def fill_weights(pairs):
    @pl.when(pl.program_id(0) == 0)
    def _():
        for main, extra, held in pairs:
            a, b = main.shape[0], extra.shape[0]
            held[:a, :] = main[...]
            held[a : a + b, :] = extra[...]
            if held.shape[0] > a + b:
                held[a + b :, :] = jnp.zeros((held.shape[0] - a - b, held.shape[1]), BF16)


def padded(main, extra):
    rows = main.shape[0] + extra.shape[0]
    return rows + -rows % 256


def down_kernel(nz, th, width, tab, *refs):
    ins = refs[:nz]
    main_ref, extra_ref, rows_ref, prod_ref, mask_ref, down_ref = refs[nz:]
    fill_weights([(main_ref, extra_ref, down_ref)])
    for z in range(nz):
        rows_ref[0, z * th : (z + 1) * th, :] = ins[z][0, 0, :, :width]
        mask_ref[0, z * th : (z + 1) * th, :] = ins[z][0, 0, :, width:]
    prod_ref[0] = dot_nt(rows_ref[0], down_ref[...])


def down_call(gathered, table, down, th, width):
    nz, count = table.shape[0] // 2, table.shape[1]
    rows = nz * th
    full_width = gathered.shape[-1]
    hid = padded(*down)

    def spec(z):
        return pl.BlockSpec(
            (1, 1, th, full_width), lambda i, tab: (tab[z, i], tab[nz + z, i], 0, 0)
        )

    step = lambda w: pl.BlockSpec((1, rows, w), lambda i, tab: (i, 0, 0))
    whole = lambda a: pl.BlockSpec(a.shape, lambda i, tab: (0, 0), pipeline_mode=pl.Buffered(1))
    return pl.pallas_call(
        functools.partial(down_kernel, nz, th, width),
        grid_spec=pltpu.PrefetchScalarGridSpec(
            num_scalar_prefetch=1,
            grid=(count,),
            in_specs=[spec(z) for z in range(nz)]
            + [whole(a) for a in down],
            out_specs=[step(width), step(hid), step(LANES)],
            scratch_shapes=[pltpu.VMEM((hid, width), BF16)],
        ),
        out_shape=[
            jax.ShapeDtypeStruct((count, rows, width), BF16),
            jax.ShapeDtypeStruct((count, rows, hid), F32),
            jax.ShapeDtypeStruct((count, rows, LANES), BF16),
        ],
        compiler_params=pltpu.CompilerParams(vmem_limit_bytes=48 * MEGA),
        cost_estimate=pl.CostEstimate(
            flops=2 * count * rows * hid * width,
            bytes_accessed=count * rows * (4 * width + 4 * hid) + 2 * hid * width,
            transcendentals=0,
        ),
        name="down_rows",
    )(table, *([gathered] * nz), *down)


def chain_kernel(arrays, th, nz, routed, tile, tab, *refs):
    ins = refs[:arrays]
    prod_ref, mask_ref, gate_a, gate_b, up_a, up_b, router_ref = refs[arrays : arrays + 7]
    outs = refs[arrays + 7 : 2 * arrays + 7]
    rows_ref, pg_ref, pu_ref, gh_ref, held, gate_ref, up_ref = refs[2 * arrays + 7 :]
    fill_weights([(gate_a, gate_b, gate_ref), (up_a, up_b, up_ref)])
    i = pl.program_id(0)
    for k in range(arrays):

        @pl.when(tab[arrays, i] == k)
        def _(k=k):
            for z in range(nz):
                rows_ref[0, z * th : (z + 1) * th, :] = ins[k][0, z]

    x = rows_ref[0]
    width = x.shape[1]
    hid = gate_ref.shape[0]
    own = tab[arrays + 1, 0]
    scores = jax.nn.sigmoid(jnp.dot(x, router_ref[...], preferred_element_type=F32))
    chosen = scores * mask_ref[0].astype(F32)
    lane = lax.broadcasted_iota(jnp.int32, chosen.shape, 1)
    mine = jnp.sum(jnp.where(lane == own, chosen, 0.0), axis=1, keepdims=True)
    gate = ROUTE_SCALE * mine / jnp.sum(chosen, axis=1, keepdims=True)
    on = jnp.sum(
        jnp.where(lane == own, mask_ref[0].astype(F32), 0.0), axis=1, keepdims=True
    )
    gate_grad = None
    for j in range(0, hid, tile):
        sl = slice(j, j + tile)
        pre_gate = dot_nt(x, gate_ref[sl, :])
        pre_up = dot_nt(x, up_ref[sl, :])
        prod = prod_ref[0, :, sl]
        sig = jax.nn.sigmoid(pre_gate)
        act = pre_gate * sig
        hidden = act * pre_up
        scale = gate
        part = hidden * prod
        if j + tile > routed:
            column = j + lax.broadcasted_iota(jnp.int32, part.shape, 1)
            scale = jnp.where(column < routed, gate, 1.0)
            part = jnp.where(column < routed, part, 0.0)
        part = jnp.sum(part, axis=1, keepdims=True)
        gate_grad = part if gate_grad is None else gate_grad + part
        upstream = prod * scale
        pg_ref[0, :, sl] = (upstream * pre_up * (sig + act * (1.0 - sig))).astype(BF16)
        pu_ref[0, :, sl] = (upstream * act).astype(BF16)
        gh_ref[0, :, sl] = (hidden * scale).astype(BF16)
    grad = jnp.dot(pg_ref[0], gate_ref[...], preferred_element_type=F32) + jnp.dot(
        pu_ref[0], up_ref[...], preferred_element_type=F32
    )
    held[:, :width] = grad.astype(BF16)
    held[:, width:] = jnp.where(lane == own, gate_grad * on, 0.0).astype(BF16)
    for k in range(arrays):

        @pl.when(tab[arrays, i] == k)
        def _(k=k):
            for z in range(nz):
                outs[k][0, z] = held[z * th : (z + 1) * th, :]


def chain_call(bufs, first, prod, mask, gate, up, router_pad, own, routed, tie):
    arrays = len(bufs)
    steps = [(k, a) for k, buf in enumerate(bufs) for a in range(buf.shape[0])]
    count = len(steps)
    nz, th, width = bufs[0].shape[1:]
    rows = nz * th
    hid = padded(*gate)
    table = np.zeros((arrays + 1, count), np.int32)
    for j in range(arrays):
        table[j] = fill_back([a if k == j else None for k, a in steps])
    table[arrays] = [k for k, _ in steps]
    tab = jnp.concatenate(
        [jnp.asarray(table), jnp.full((1, count), 1, jnp.int32) * own.astype(jnp.int32)], axis=0
    )
    tab = after(tab, tie)
    wide = width + LANES

    def block(j, w):
        return pl.BlockSpec((1, nz, th, w), lambda i, tab: (tab[j, i], 0, 0, 0))

    step = lambda w, base=0: pl.BlockSpec((1, rows, w), lambda i, tab: (i + base, 0, 0))
    whole = lambda a: pl.BlockSpec(a.shape, lambda i, tab: (0, 0), pipeline_mode=pl.Buffered(1))
    return pl.pallas_call(
        functools.partial(chain_kernel, arrays, th, nz, routed, 256),
        grid_spec=pltpu.PrefetchScalarGridSpec(
            num_scalar_prefetch=1,
            grid=(count,),
            in_specs=[block(j, width) for j in range(arrays)]
            + [step(hid, first), step(LANES, first)]
            + [whole(a) for a in (*gate, *up, router_pad)],
            out_specs=[block(j, wide) for j in range(arrays)]
            + [step(width), step(hid), step(hid), step(hid)],
            scratch_shapes=[pltpu.VMEM((rows, wide), BF16)]
            + [pltpu.VMEM((hid, width), BF16)] * 2,
        ),
        out_shape=[jax.ShapeDtypeStruct((*buf.shape[:3], wide), BF16) for buf in bufs]
        + [jax.ShapeDtypeStruct((count, rows, width), BF16)]
        + [jax.ShapeDtypeStruct((count, rows, hid), BF16)] * 3,
        compiler_params=pltpu.CompilerParams(vmem_limit_bytes=56 * MEGA),
        cost_estimate=pl.CostEstimate(
            flops=8 * count * rows * hid * width,
            bytes_accessed=count * rows * (6 * width + 10 * hid) + 4 * hid * width,
            transcendentals=count * rows * hid,
        ),
        name="expert_chain",
    )(tab, *bufs, prod, mask, *gate, *up, router_pad)


def out_kernel(arrays, th, nz, tab, gh_ref, main_ref, extra_ref, *refs):
    outs, held, down_ref = refs[:arrays], refs[arrays], refs[arrays + 1]
    fill_weights([(main_ref, extra_ref, down_ref)])
    i = pl.program_id(0)
    held[...] = jnp.dot(gh_ref[0], down_ref[...], preferred_element_type=F32).astype(BF16)
    for k in range(arrays):

        @pl.when(tab[arrays, i] == k)
        def _(k=k):
            for z in range(nz):
                outs[k][0, z] = held[z * th : (z + 1) * th, :]


def out_call(gated, down, shapes, tie):
    arrays = len(shapes)
    steps = [(k, a) for k, shape in enumerate(shapes) for a in range(shape[0])]
    count = len(steps)
    _, nz, th, width = shapes[0]
    rows = nz * th
    hid = padded(*down)
    table = np.zeros((arrays + 1, count), np.int32)
    for j in range(arrays):
        table[j] = fill_back([a if k == j else None for k, a in steps])
    table[arrays] = [k for k, _ in steps]

    def block(j):
        return pl.BlockSpec((1, nz, th, width), lambda i, tab: (tab[j, i], 0, 0, 0))

    return pl.pallas_call(
        functools.partial(out_kernel, arrays, th, nz),
        grid_spec=pltpu.PrefetchScalarGridSpec(
            num_scalar_prefetch=1,
            grid=(count,),
            in_specs=[
                pl.BlockSpec((1, rows, hid), lambda i, tab: (i, 0, 0)),
            ]
            + [
                pl.BlockSpec(a.shape, lambda i, tab: (0, 0), pipeline_mode=pl.Buffered(1))
                for a in down
            ],
            out_specs=[block(j) for j in range(arrays)],
            scratch_shapes=[pltpu.VMEM((rows, width), BF16), pltpu.VMEM((hid, width), BF16)],
        ),
        out_shape=[jax.ShapeDtypeStruct(shape, BF16) for shape in shapes],
        compiler_params=pltpu.CompilerParams(vmem_limit_bytes=48 * MEGA),
        cost_estimate=pl.CostEstimate(
            flops=2 * count * rows * hid * width,
            bytes_accessed=count * rows * 2 * (width + hid) + 2 * hid * width,
            transcendentals=0,
        ),
        name="expert_out",
    )(after(jnp.asarray(table), tie), gated, *down)


def weight_kernel(calls, per, outs_n, hid, extra, tie_ref, *refs):
    lefts, rights = refs[: calls * outs_n], refs[calls * outs_n : calls * (outs_n + 1)]
    outs = refs[calls * (outs_n + 1) :]
    i = pl.program_id(0)

    @pl.when(i == 0)
    def _():
        for o in outs:
            o[...] = jnp.zeros_like(o)

    for c in range(calls):

        @pl.when(i // per == c)
        def _(c=c):
            right = rights[c][0]
            for k in range(outs_n):
                full = lax.dot_general(
                    lefts[k * calls + c][0],
                    right,
                    (((0,), (0,)), ((), ())),
                    preferred_element_type=F32,
                )
                outs[k][...] += full[:hid]
                outs[outs_n + k][...] += full[hid : hid + extra]


def weight_call(lefts, rights, hid, extra, tie):
    calls, outs_n = len(rights), len(lefts)
    bases = [r[1] if len(r) > 1 else 0 for r in rights]
    rights = [r[0] for r in rights]
    per, rows, pad = lefts[0][0].shape
    width = rights[0].shape[2]
    if per % 2 == 0 and rows <= 256:
        rights = [r.reshape(r.shape[0] // 2, 2 * rows, width) for r in rights]
        lefts = [[a.reshape(per // 2, 2 * rows, pad) for a in left] for left in lefts]
        per, rows, bases = per // 2, 2 * rows, [base // 2 for base in bases]

    def spec(c, w, base=0):
        return pl.BlockSpec(
            (1, rows, w), lambda i: (base + jnp.clip(i - c * per, 0, per - 1), 0, 0)
        )

    return pl.pallas_call(
        functools.partial(weight_kernel, calls, per, outs_n, hid, extra),
        grid=(calls * per,),
        in_specs=[pl.BlockSpec(memory_space=pl.ANY)]
        + [spec(c, pad) for _ in range(outs_n) for c in range(calls)]
        + [spec(c, width, bases[c]) for c in range(calls)],
        out_specs=[pl.BlockSpec((hid, width), lambda i: (0, 0))] * outs_n
        + [pl.BlockSpec((extra, width), lambda i: (0, 0))] * outs_n,
        out_shape=[jax.ShapeDtypeStruct((hid, width), F32)] * outs_n
        + [jax.ShapeDtypeStruct((extra, width), F32)] * outs_n,
        compiler_params=pltpu.CompilerParams(vmem_limit_bytes=58 * MEGA),
        cost_estimate=pl.CostEstimate(
            flops=2 * outs_n * calls * per * rows * pad * width,
            bytes_accessed=calls * per * rows * 2 * (outs_n * pad + width) + 4 * outs_n * hid * width,
            transcendentals=0,
        ),
        name="expert_weights",
    )(after(jnp.zeros((8, LANES), F32), tie), *[a for left in lefts for a in left], *rights)


def rotary_tables(segment_row):
    length = segment_row.shape[-1]
    places = jnp.arange(length, dtype=jnp.int32)
    same_document = segment_row[:, :, None] == segment_row[:, None, :]
    position = jnp.sum(
        jnp.where(same_document & (places[None, :] < places[:, None])[None], 1.0, 0.0), axis=2
    )
    half_rope = ROPE // 2
    frequency = ROTARY_BASE ** (-2.0 * jnp.arange(half_rope, dtype=F32) / ROPE)
    angles = position[:, :, None] * frequency
    cosine = jnp.concatenate([jnp.cos(angles), jnp.cos(angles)], axis=-1)
    sine_table = jnp.concatenate([jnp.sin(angles), jnp.sin(angles)], axis=-1)
    allowed = same_document & (places[None, :] <= places[:, None])[None]
    return cosine, sine_table, allowed


def rotate(values, cosine, sine_table):
    half_rope = values.shape[-1] // 2
    turned = jnp.concatenate([-values[..., half_rope:], values[..., :half_rope]], axis=-1)
    return values * cosine + turned * sine_table


def unrotate(upstream, cosine, sine_table):
    half_rope = upstream.shape[-1] // 2
    weighted = upstream * sine_table
    turned = jnp.concatenate([weighted[..., half_rope:], -weighted[..., :half_rope]], axis=-1)
    return upstream * cosine + turned


def einsum(pattern, a, b):
    return jnp.einsum(pattern, a, b, preferred_element_type=F32)


def body(
    tokens,
    segment_ids,
    routes,
    attn_gain,
    w_query,
    w_latent,
    latent_gain,
    w_keyval,
    w_output,
    ffn_gain,
    w_router,
    shared_gate,
    shared_up,
    shared_down,
    expert_gate,
    expert_up,
    expert_down,
    cotangent,
):
    net = Net()
    S, E, s, e = net.S, net.E, net.s, net.e
    T, D = tokens.shape
    DK = D // S
    HL = HEADS // S
    HQ = HL * (NOPE + ROPE)
    HV = HL * (NOPE + VDIM)
    HID = shared_down.shape[0]
    blocks = list(range(S))

    def cols(value, index, size):
        return lax.dynamic_slice_in_dim(value, (index % S) * size, size, value.ndim - 1)

    def pair_rows(value):
        return jnp.stack(net.ring_gather(value, "y"), axis=0)

    def pair_sum_blocks(parts):
        total = parts[0].astype(F32)
        for r in range(1, S):
            total = total + net.hop(parts[r].astype(BF16), "y", r).astype(F32)
        return total

    KR = KVR // S
    packed = jnp.concatenate(
        [
            w_router.T,
            ffn_gain[None],
            jnp.pad(latent_gain, (0, DK - KR))[None],
        ],
        axis=0,
    )
    packed = net.ring_gather(packed, "y")
    router_full = net.absolute([p[:E] for p in packed], "y", 1)
    ffn_gain_full = net.absolute([p[E] for p in packed], "y", 0).astype(F32)
    latent_gain_full = net.absolute([p[E + 1, :KR] for p in packed], "y", 0).astype(F32)
    inputs = tokens.astype(F32)
    scale_one = norm_scale(inputs)
    rows2 = jnp.concatenate([segment_ids.astype(F32), scale_one.reshape(1, T)], axis=0)
    rows2 = jnp.stack(net.ring_gather(rows2, "y"), axis=0)
    seg_pair = rows2[:, 0]
    scales = rows2[:, 1].reshape(S, T, 1)
    x_pieces = [cols(tokens, s, DK)] + [None] * (S - 1)
    for r in range(1, S):
        x_pieces[S - r] = net.hop(cols(tokens, s + r, DK), "y", r)
    x_cols = jnp.stack(x_pieces, axis=0).astype(F32)
    attn_gain_f = attn_gain.astype(F32)
    plain_one = x_cols * scales
    normed_one = (plain_one * attn_gain_f).astype(BF16).reshape(S * T, DK)
    cosine, sine_table, allowed = rotary_tables(seg_pair)

    query_parts = [
        dot(normed_one, cols(w_query, s + r, HQ)).astype(BF16).reshape(S, T, HQ)
        for r in range(1, S)
    ]
    latent_part_own = dot(normed_one, w_latent).reshape(S, T, -1)
    latent_sent = latent_part_own.astype(BF16)
    first = (query_parts, latent_sent)
    query_got = [net.hop(part, "y", r) for r, part in enumerate(query_parts, 1)]
    latent_got = [net.hop(latent_sent, "y", r) for r in range(1, S)]
    core = net.pos("c")
    half_rows = KR // net.n["c"]
    kv_half = lax.dynamic_slice_in_dim(w_keyval, core * half_rows, half_rows, 0)
    kv_pieces = [cols(w_keyval, s, HV)] + [None] * (S - 1)
    for r in range(1, S):
        got = net.hop(after(cols(kv_half, s + r, HV), first), "y", r)
        kv_pieces[S - r] = net.absolute(net.ring_gather(got, "c"), "c", 0)
    keyval_full = net.absolute(kv_pieces, "y", 0)

    HS = HID // E
    HP = -(-HS // 16) * 16
    sh_pieces = [None] * S
    for r in range(S):
        mine = [
            lax.dynamic_slice_in_dim(w, ((s + r) % S) * HID + e * HS, HS, 1).T
            for w in (shared_gate, shared_up)
        ]
        mine = jnp.pad(jnp.stack(mine, axis=0), ((0, 0), (0, HP - HS), (0, 0)))
        mine = after(mine, first)
        sh_pieces[(S - r) % S] = net.hop(mine, "y", r) if r else mine
    sh_slices = net.absolute(sh_pieces, "y", 2)
    sh_down = lax.dynamic_slice_in_dim(shared_down, e * HS, HS, 0)
    sh_down = after(jnp.pad(sh_down, ((0, HP - HS), (0, 0))), first)
    down_t = (expert_down[0], sh_down)
    gate_t = (expert_gate[0].T, sh_slices[0])
    up_t = (expert_up[0].T, sh_slices[1])
    router_pad = jnp.pad(router_full.T, ((0, 0), (0, LANES - E)))

    queries = dot(normed_one, cols(w_query, s, HQ)).reshape(S, T, HQ)
    queries = after(queries, sh_down, sh_slices, keyval_full)
    for r, got in enumerate(query_got, 1):
        queries = queries + jnp.concatenate([got[r:], got[:r]], axis=0).astype(F32)
    queries = queries.reshape(S, T, HL, NOPE + ROPE)

    def block_all_sum(value):
        total = value
        for r in range(1, S):
            got = net.hop(value.astype(BF16), "y", r).astype(F32)
            total = total + jnp.concatenate([got[r:], got[:r]], axis=0)
        return total

    latent_all = latent_part_own
    for r, got in enumerate(latent_got, 1):
        latent_all = latent_all + jnp.concatenate([got[r:], got[:r]], axis=0).astype(F32)
    query_turn = rotate(queries[..., NOPE:], cosine[:, :, None, :], sine_table[:, :, None, :])
    query_b = jnp.concatenate([queries[..., :NOPE], query_turn], axis=-1).astype(BF16)
    latent = latent_all[..., :KVR]
    key_rope = rotate(latent_all[..., KVR:], cosine, sine_table)
    scale_latent = norm_scale(latent)
    latent_normed = (latent * scale_latent * latent_gain_full).astype(BF16)
    keyval = dot(latent_normed.reshape(S * T, KVR), keyval_full).reshape(S, T, HL, NOPE + VDIM)
    key_shared = jnp.broadcast_to(key_rope[:, :, None, :], (S, T, HL, ROPE))
    key_b = jnp.concatenate([keyval[..., :NOPE], key_shared], axis=-1).astype(BF16)
    value_b = keyval[..., NOPE:].astype(BF16)
    att_scale = (NOPE + ROPE) ** (-0.5)
    scores = einsum("bthd,bshd->bhts", query_b, key_b) * att_scale
    scores = jnp.where(allowed[:, None], scores, NEGATIVE)
    peak = jnp.max(scores, axis=-1, keepdims=True)
    raised = jnp.exp(scores - peak)
    probs = raised / jnp.sum(raised, axis=-1, keepdims=True)
    probs_b = probs.astype(BF16)
    attended = einsum("bhts,bshd->bthd", probs_b, value_b).astype(BF16).reshape(S * T, HL * VDIM)
    out_parts = dot(attended, w_output).reshape(S, T, D)
    residual = inputs + pair_sum_blocks([out_parts[r] for r in blocks])
    scale_two = norm_scale(residual)
    normed_two = (residual * scale_two * ffn_gain_full).astype(BF16)

    th = T // 2
    nx, ny, nz, nc = net.n["x"], net.n["y"], net.n["z"], net.n["c"]
    ids = jnp.arange(E, dtype=jnp.int32)
    mask_own = jnp.sum((routes[:, :, None] == ids[None, None, :]).astype(F32), axis=1)
    mask_lanes = jnp.pad(mask_own.astype(BF16), ((0, 0), (0, LANES - E)))
    cot_wide = jnp.concatenate([cotangent, mask_lanes], axis=1)
    cot_gathered = lax.all_gather(cot_wide, ("expert", "shard"), axis=0).reshape(
        E * S, 2, th, D + LANES
    )
    nr = max(nx, ny)
    steps = []
    for r in range(nr):
        for p in range(2):
            for c in range(nc):
                for k in range(nx if p == 0 else ny):
                    steps.append((k, c, r, p) if p == 0 else (r, c, k, p))
    at = {axis: net.pos(axis) for axis in "cxzy"}
    ahead = lambda axis, k: (at[axis] + jnp.asarray(k, jnp.int32)) % net.n[axis]
    step_x, step_c, step_y, step_p = [np.array(v, np.int32) for v in zip(*steps)]
    table = []
    for z in range(nz):
        expert_of = (
            ahead("z", z) * net.stride["z"]
            + ahead("x", step_x) * net.stride["x"]
            + ahead("c", step_c) * net.stride["c"]
        )
        table.append(expert_of * S + ahead("y", step_y))
    table = jnp.stack(table + [jnp.asarray(step_p)] * nz, axis=0).astype(jnp.int32)
    cot_rows, cot_prod, mask_rows = down_call(cot_gathered, table, down_t, th, D)
    tok_1 = net.gather_part(normed_two[:th], "x", mask_rows)
    tok_2 = net.gather_part(normed_two[th:], "y", mask_rows)
    per = len(steps) // nr
    in_1, in_2 = [], []
    x_rows, pg_rows, pu_rows, gh_rows = [], [], [], []
    for r in range(nr):
        if r == 0:
            bufs, tie = tok_1[0] + tok_2[0], ()
        else:
            tie = gh_rows[-1]
            far = after((tok_1[1][r - 1], tok_2[1][r - 1]), tie)
            bufs = net.ring_gather(far[0], "c") + net.ring_gather(far[1], "c")
        got = chain_call(
            bufs, r * per, cot_prod, mask_rows, gate_t, up_t, router_pad, e, HID, tie
        )
        in_1.append(got[:nc])
        in_2.append(got[nc : 2 * nc])
        x_rows.append(got[2 * nc])
        pg_rows.append(got[2 * nc + 1])
        pu_rows.append(got[2 * nc + 2])
        gh_rows.append(got[2 * nc + 3])
    in_sum_1, in_sum_2 = net.scatter_cores(in_1), net.scatter_cores(in_2)
    shapes = [buf.shape for buf in tok_1[0] + tok_2[0]]
    weight_grads, out_sums, out_bufs = {}, [], []

    def weights_of(name, rows, rights, tie):
        weight_grads[name] = weight_call([rows], rights, HID, HS, tie)
        return weight_grads[name]

    def gate_up_work(marks):
        rights = [[v] for v in x_rows]
        one = weights_of("gate", pg_rows, rights, marks)
        return [weights_of("up", pu_rows, rights, one[1])[1]]

    def down_work(marks):
        rights = [(cot_rows, r * per) for r in range(nr)]
        return weights_of("down", gh_rows, rights, marks)[1]

    def out_work(r):
        def job(marks):
            out_bufs.append(out_call(gh_rows[r], down_t, shapes, marks))
            return out_bufs[-1][0]

        return job

    def out_sum_work(marks):
        for bufs in out_bufs:
            out_sums.append([net.ring_list(bufs[:nc], "c"), net.ring_list(bufs[nc:], "c")])
        return [v[0] for v in out_sums]

    hops = max(nx, ny) - 1
    work = [gate_up_work] + [None] * (hops - 1) + [down_work] + [None] * (hops - 1)
    early = min(nr, nz - 2)
    work += [out_work(r) for r in range(early)]
    if early == nr:
        work.append(out_sum_work)
    in_wide = net.scatter_both(in_sum_1, in_sum_2, work)
    gate_w_grad, sh_gate_rows = weight_grads["gate"]
    up_w_grad, sh_up_rows = weight_grads["up"]
    down_grad, sh_down_rows = weight_grads["down"]
    in_grad = in_wide[:, :D]
    gate_grads_raw = in_wide[:, D : D + E].astype(F32)

    def gather_cols(value, width):
        pieces = [value.reshape(S, T, width)] + [None] * (S - 1)
        for r in range(1, S):
            got = net.hop(value.reshape(S, T, width), "y", r)
            pieces[S - r] = jnp.concatenate([got[r:], got[:r]], axis=0)
        return net.absolute(pieces, "y", 2).reshape(S * T, S * width)

    def own_cols(value):
        pieces = [value[0].astype(BF16)] + [None] * (S - 1)
        for r in range(1, S):
            pieces[S - r] = net.hop(value[r].astype(BF16), "y", r)
        return net.absolute(pieces, "y", 1).astype(F32)

    scores_own = jax.nn.sigmoid(dot_tr(normed_two, router_full))
    gate_grads = gate_grads_raw * mask_own
    picked = scores_own * mask_own
    picked_total = jnp.sum(picked, axis=1, keepdims=True)
    weighted = jnp.sum(gate_grads * picked, axis=1, keepdims=True)
    picked_grad = ROUTE_SCALE * (
        gate_grads / picked_total - weighted / (picked_total * picked_total)
    )
    logit_grad_b = (picked_grad * picked * (1.0 - picked)).astype(BF16)
    normed_two_grad = in_grad.astype(F32) + dot(logit_grad_b, router_full)
    upstream = cotangent.astype(F32)
    plain_two = residual * scale_two
    ffn_gain_part = jnp.sum(normed_two_grad * plain_two, axis=0)
    inner = normed_two_grad * ffn_gain_full
    residual_grad = upstream + scale_two * (
        inner - plain_two * jnp.mean(inner * plain_two, axis=-1, keepdims=True)
    )
    router_grad_part = dot_tl(normed_two, logit_grad_b)

    room = ((0, HP - HS), (0, 0))
    sh_gu = jnp.stack([jnp.pad(v.astype(BF16), room) for v in (sh_gate_rows, sh_up_rows)], axis=0)
    sh_down_own = jnp.pad(sh_down_rows.astype(BF16), room)
    gu_pieces = [None] * S
    for r in range(S):
        piece = cols(sh_gu, s + r, DK)
        gu_pieces[(S - r) % S] = net.hop(piece, "y", r) if r else piece
    gu_own = net.absolute([piece[:, None] for piece in gu_pieces], "y", 1).reshape(2 * S * HP, DK)
    gu_all = lax.all_gather(gu_own, "expert", axis=0, tiled=True)
    down_all = lax.all_gather(sh_down_own, "expert", axis=0, tiled=True)

    grad_b = net.ring_gather(residual_grad.astype(BF16), "y")
    grad_b = jnp.stack(grad_b, axis=0).reshape(S * T, D)
    output_part = dot_tl(attended, grad_b)
    attended_grad = dot_tr(grad_b, w_output).astype(BF16).reshape(S, T, HL, VDIM)
    value_grad = einsum("bhts,bthd->bshd", probs_b, attended_grad)
    probs_grad = einsum("bthd,bshd->bhts", attended_grad, value_b)
    center = jnp.sum(probs * probs_grad, axis=-1, keepdims=True)
    output_part = after(output_part, gu_all, down_all).astype(BF16)
    output_w = lax.psum(output_part, "expert")
    scores_grad = (after(probs, output_part) * (probs_grad - center) * att_scale).astype(BF16)
    query_grad = einsum("bhts,bshd->bthd", scores_grad, key_b)
    key_grad = einsum("bhts,bthd->bshd", scores_grad, query_b)
    query_turn_grad = unrotate(
        query_grad[..., NOPE:], cosine[:, :, None, :], sine_table[:, :, None, :]
    )
    query_grad_b = (
        jnp.concatenate([query_grad[..., :NOPE], query_turn_grad], axis=-1)
        .astype(BF16)
        .reshape(S * T, HQ)
    )
    query_grad_all = gather_cols(query_grad_b, HQ)
    if not out_sums:
        for r in range(early, nr):
            out_work(r)(query_grad_b)
        out_sum_work(())
    keyval_grad_b = (
        jnp.concatenate([key_grad[..., :NOPE], value_grad], axis=-1)
        .astype(BF16)
        .reshape(S * T, HV)
    )
    latent_part = dot_tr(keyval_grad_b, keyval_full).reshape(S, T, KVR)
    rope_part = jnp.sum(key_grad[..., NOPE:], axis=2)
    latent_sum = block_all_sum(jnp.concatenate([latent_part, rope_part], axis=-1))
    latent_up = latent_sum[..., :KVR]
    key_rope_grad = unrotate(latent_sum[..., KVR:], cosine, sine_table)
    plain_latent = latent * scale_latent
    latent_gain_part = jnp.sum(latent_up * plain_latent, axis=(0, 1))
    inner_latent = latent_up * latent_gain_full
    latent_grad = scale_latent * (
        inner_latent - plain_latent * jnp.mean(inner_latent * plain_latent, axis=-1, keepdims=True)
    )
    latent_all_grad = (
        jnp.concatenate([latent_grad, key_rope_grad], axis=-1).astype(BF16).reshape(S * T, -1)
    )
    normed_grad = dot_tr(query_grad_all, w_query) + dot_tr(latent_all_grad, w_latent)
    plain_flat = plain_one.reshape(S * T, DK)
    attn_gain_part = jnp.sum(normed_grad * plain_flat, axis=0)
    inner_one = own_cols((normed_grad * attn_gain_f).reshape(S, T, DK))
    plain_own = inputs * scale_one
    tokens_grad = residual_grad + scale_one * (
        inner_one - plain_own * jnp.mean(inner_one * plain_own, axis=-1, keepdims=True)
    )

    query_part = dot_tl(normed_one, query_grad_all).astype(BF16)
    ffn_part, router_part = after((ffn_gain_part, router_grad_part), query_part)
    small_ffn = cols(ffn_part, s, DK)
    small_router = cols(router_part.T, s, DK)
    for r in range(1, S):
        sent = jnp.concatenate(
            [cols(ffn_part, s + r, DK)[None], cols(router_part.T, s + r, DK)], axis=0
        )
        got = net.hop(sent, "y", r)
        small_ffn = small_ffn + got[0]
        small_router = small_router + got[1:]
    latent_rows = dot_tl(latent_all_grad, normed_one).astype(BF16)
    small = jnp.concatenate(
        [
            attn_gain_part[None],
            small_ffn[None],
            jnp.pad(cols(latent_gain_part, s, KR), (0, DK - KR))[None],
            small_router,
        ],
        axis=0,
    )
    LW = latent_rows.shape[0]
    xz = ("c", "x", "z")
    output_w = output_w.astype(F32)
    tot_q, tot_l = lax.psum((query_part, latent_rows), "expert")
    tot_s = small
    for axis in "cxz":
        pieces = net.ring_gather(tot_s, axis)
        tot_s = functools.reduce(jnp.add, pieces)

    row_ids = after(jnp.arange(E * 2 * S * HP, dtype=jnp.int32), query_part)
    at_hidden = (
        ((row_ids // (HP * S)) % 2) * (S * HID)
        + ((row_ids // HP) % S) * HID
        + (row_ids // (HP * S * 2)) * HS
        + row_ids % HP
    )
    at_hidden = jnp.where(row_ids % HP < HS, at_hidden, -1)
    hidden_ids = jnp.arange(S * HID, dtype=jnp.int32)
    shared_gate_w = dot_tl(gu_all, (at_hidden[:, None] == hidden_ids[None]).astype(BF16))
    shared_up_w = dot_tl(gu_all, (at_hidden[:, None] == S * HID + hidden_ids[None]).astype(BF16))
    row_ids = after(jnp.arange(E * HP, dtype=jnp.int32), query_part)
    at_hidden = jnp.where(row_ids % HP < HS, (row_ids // HP) * HS + row_ids % HP, -1)
    place_down = (jnp.arange(HID, dtype=jnp.int32)[:, None] == at_hidden[None]).astype(BF16)
    shared_down_w = dot(place_down, down_all)

    def keyval_steps():
        piece = dot_tl(keyval_grad_b, latent_normed.reshape(S * T, KVR))
        piece = after(piece, query_part).astype(BF16)
        piece = yield from net.reduce_steps(piece, xz)
        mine = [cols(piece, s, KR)] + [None] * (S - 1)
        for r in range(1, S):
            mine[S - r] = net.hop(cols(piece, s + r, KR), "y", r)
        mine = net.absolute([p[None] for p in mine], "y", 0)
        value = yield from net.spread_steps(mine, xz, dim=1)
        return value

    out_1, out_2 = [v[0] for v in out_sums], [v[1] for v in out_sums]
    split = lambda v: [v[k] for k in range(v.shape[0])]
    got = net.scatter_stage(
        [split(v) for v in out_1] + [out_2],
        ("x",) * (len(out_1) + 1),
        [lambda marks: query_part] + [None] * (nx - 2),
    )
    one, two = net.scatter_stage([got[:-1], split(got[-1])], ("y", "y"))
    one = [jnp.concatenate([one[k], two[k]], axis=0) for k in range(nz)]
    routed = net.scatter_stage([one], ("z",))[0].astype(F32)
    (kv_all,) = net.in_rounds([keyval_steps()])
    block_out = (residual + routed).astype(BF16)
    keyval_w = dot_tr(jnp.eye(KR, dtype=BF16), kv_all.reshape(S * HV, KR))
    query_w = tot_q.astype(F32)
    latent_w = tot_l.astype(F32).T
    return (
        block_out,
        tokens_grad,
        tot_s[0],
        query_w,
        latent_w,
        tot_s[2, :KR],
        keyval_w,
        output_w,
        tot_s[1],
        tot_s[3:].T,
        shared_gate_w,
        shared_up_w,
        shared_down_w,
        gate_w_grad.T[None],
        up_w_grad.T[None],
        down_grad[None],
    )


def solution(mesh):
    both = P(("expert", "shard"), None)
    row = P("shard", None)
    in_specs = (
        both, both, both, P("shard"), row, row, P("shard"), row, row, P("shard"), row, row, row, row,
        P("expert", None, "shard"), P("expert", None, "shard"), P("expert", "shard", None), both,
    )
    out_specs = (
        both, both, P("shard"), row, row, P("shard"), row, row, P("shard"), row, row, row, row,
        P("expert", None, "shard"), P("expert", None, "shard"), P("expert", "shard", None),
    )
    return jax.shard_map(body, mesh=mesh, in_specs=in_specs, out_specs=out_specs, check_vma=False)
```

```python
import functools

import jax
import jax.numpy as jnp
import numpy as np
from jax import lax
from jax.experimental import pallas as pl
from jax.experimental.pallas import tpu as pltpu
from jax.sharding import PartitionSpec as P

HEADS = 16
NOPE = 128
ROPE = 64
VDIM = 128
KVR = 512
NORM_EPSILON = 1e-06
ROTARY_BASE = 50000.0
ROUTE_SCALE = 2.446
NEGATIVE = -1e30
F32 = jnp.float32
BF16 = jnp.bfloat16


def dot(a, b):
    return jnp.dot(a, b, preferred_element_type=F32)


def dot_tl(a, b):
    return lax.dot_general(a, b, (((0,), (0,)), ((), ())), preferred_element_type=F32)


def dot_tr(a, b):
    return lax.dot_general(a, b, (((1,), (1,)), ((), ())), preferred_element_type=F32)


def norm_scale(values):
    return lax.rsqrt(jnp.mean(values * values, axis=-1, keepdims=True) + NORM_EPSILON)


def zero_of(*marks):
    total = jnp.zeros((), F32)
    for mark in jax.tree.leaves(marks):
        one = lax.slice(mark, (0,) * mark.ndim, (1,) * mark.ndim).reshape(())
        total = total + (one != one).astype(F32)
    return total


def after(value, *marks):
    zero = zero_of(*marks)
    return jax.tree.map(lambda v: v + zero.astype(v.dtype), value)


def add_b(a, b):
    return (a.astype(F32) + b.astype(F32)).astype(BF16)


class Net:
    def __init__(self):
        self.E = lax.axis_size("expert")
        self.S = lax.axis_size("shard")
        nx = self.S if self.E % (2 * self.S) == 0 else 1
        nc = 2 if self.E % 2 == 0 else 1
        self.n = {"c": nc, "x": nx, "z": self.E // (nc * nx), "y": self.S}
        self.stride = {"c": 1, "x": nc, "z": nc * nx}
        self.e = lax.axis_index("expert")
        self.s = lax.axis_index("shard")

    def pos(self, axis):
        if axis == "y":
            return self.s
        return (self.e // self.stride[axis]) % self.n[axis]

    def hop(self, value, axis, k=1):
        n = self.n[axis]
        if axis == "y":
            return lax.ppermute(value, "shard", [(i, (i + k) % n) for i in range(n)])
        st = self.stride[axis]
        pairs = []
        for i in range(self.E):
            p = (i // st) % n
            pairs.append((i, i + ((p + k) % n - p) * st))
        return lax.ppermute(value, "expert", pairs)

    def ring_gather(self, value, axis):
        n = self.n[axis]
        out = [None] * n
        out[0] = value
        cur = value
        for k in range(1, n):
            cur = self.hop(cur, axis)
            out[n - k] = cur
        return out

    def ring_scatter(self, value, axis, dim, add):
        n = self.n[axis]
        take = lambda r: lax.index_in_dim(value, r, dim, keepdims=False)
        acc = take(n - 1)
        for k in range(1, n):
            acc = add(take(n - 1 - k), self.hop(acc, axis))
        return acc

    def absolute(self, pieces, axis, dim):
        n = self.n[axis]
        i = self.pos(axis)
        if n == 1:
            return pieces[0]
        if n == 2:
            first = jnp.concatenate(pieces, axis=dim)
            second = jnp.concatenate(pieces[::-1], axis=dim)
            return jnp.where(i == 0, first, second)
        size = pieces[0].shape[dim]
        twice = jnp.concatenate(list(pieces) * 2, axis=dim)
        return lax.dynamic_slice_in_dim(twice, ((n - i) % n) * size, n * size, dim)

    def gather_part(self, value, mid, mark):
        last = "y" if mid == "x" else "x"
        cur = jnp.stack(self.ring_gather(value, "z"), axis=0)
        pieces = self.ring_gather(cur, mid)
        cur = jnp.stack(pieces[:1] + after(pieces[1:], mark), axis=0)
        return self.ring_gather(cur, "c"), self.ring_gather(cur, last)[1:]

    def scatter_cores(self, bufs):
        return [self.ring_list(pieces, "c") for pieces in bufs]

    def scatter_stage(self, lists, axes, work=None):
        n = max(self.n[axis] for axis in axes)
        accs = [pieces[self.n[axis] - 1] for pieces, axis in zip(lists, axes)]
        for k in range(1, n):
            got = [
                self.hop(acc, axis) if k < self.n[axis] else None for acc, axis in zip(accs, axes)
            ]
            job = None
            if work:
                job = work.pop(0)
            if job is not None:
                mark = job(accs)
                got = [g if g is None else after(g, mark) for g in got]
            accs = [
                acc if g is None else add_b(pieces[self.n[axis] - 1 - k], g)
                for acc, g, pieces, axis in zip(accs, got, lists, axes)
            ]
        return accs

    def scatter_both(self, sums_1, sums_2, work=None):
        work = list(work or [])
        split = lambda v: [v[k] for k in range(v.shape[0])]
        one, two = self.scatter_stage([sums_1, sums_2], ("y", "x"), work)
        one, two = self.scatter_stage([split(one), split(two)], ("x", "y"), work)
        rows = [jnp.concatenate([one[k], two[k]], axis=0) for k in range(self.n["z"])]
        return self.scatter_stage([rows], ("z",), work)[0]

    def ring_list(self, pieces, axis):
        n = self.n[axis]
        acc = pieces[n - 1]
        for k in range(1, n):
            acc = add_b(pieces[n - 1 - k], self.hop(acc, axis))
        return acc

    def reduce_steps(self, value, order):
        for axis in order:
            n, i = self.n[axis], self.pos(axis)
            if n == 1:
                continue
            rows = value.shape[0] // n
            take = lambda k, v=value: lax.dynamic_slice_in_dim(v, (k % n) * rows, rows, 0)
            got = yield [(take(i + k), axis, k) for k in range(1, n)]
            total = take(i).astype(F32)
            for piece in got:
                total = total + piece.astype(F32)
            value = total.astype(BF16)
        return value

    def spread_steps(self, value, order, dim=0):
        for axis in order[::-1]:
            n = self.n[axis]
            if n == 1:
                continue
            got = yield [(value, axis, k) for k in range(1, n)]
            value = self.absolute([value] + list(got)[::-1], axis, dim)
        return value

    def total_steps(self, value, order):
        value = yield from self.reduce_steps(value, order)
        value = yield from self.spread_steps(value, order)
        return value

    def in_rounds(self, runs):
        results = [None] * len(runs)
        sends = {k: next(run) for k, run in enumerate(runs)}
        while sends:
            keys = [k for k in sends if sends[k]]
            values = [[v[0] for v in sends[k]] for k in keys]
            got = {
                k: [self.hop(v, item[1], item[2]) for v, item in zip(vs, sends[k])]
                for k, vs in zip(keys, values)
            }
            following = {}
            for k in sends:
                try:
                    following[k] = runs[k].send(got.get(k))
                except StopIteration as stop:
                    results[k] = stop.value
            sends = following
        return results


MEGA = 2**20
LANES = 128


def dot_nt(a, b):
    return lax.dot_general(a, b, (((1,), (1,)), ((), ())), preferred_element_type=F32)


def fill_back(entries):
    out = list(entries)
    for i in reversed(range(len(out) - 1)):
        if out[i] is None:
            out[i] = out[i + 1]
    last = None
    for i in range(len(out)):
        last = out[i] if out[i] is not None else last
        out[i] = last
    return out


def fill_weights(pairs):
    @pl.when(pl.program_id(0) == 0)
    def _():
        for main, extra, held in pairs:
            a, b = main.shape[0], extra.shape[0]
            held[:a, :] = main[...]
            held[a : a + b, :] = extra[...]
            if held.shape[0] > a + b:
                held[a + b :, :] = jnp.zeros((held.shape[0] - a - b, held.shape[1]), BF16)


def padded(main, extra):
    rows = main.shape[0] + extra.shape[0]
    return rows + -rows % 256


def down_kernel(nz, th, width, tab, *refs):
    ins = refs[:nz]
    main_ref, extra_ref, rows_ref, prod_ref, mask_ref, down_ref = refs[nz:]
    fill_weights([(main_ref, extra_ref, down_ref)])
    for z in range(nz):
        rows_ref[0, z * th : (z + 1) * th, :] = ins[z][0, 0, :, :width]
        mask_ref[0, z * th : (z + 1) * th, :] = ins[z][0, 0, :, width:]
    prod_ref[0] = dot_nt(rows_ref[0], down_ref[...])


def down_call(gathered, table, down, th, width):
    nz, count = table.shape[0] // 2, table.shape[1]
    rows = nz * th
    full_width = gathered.shape[-1]
    hid = padded(*down)

    def spec(z):
        return pl.BlockSpec(
            (1, 1, th, full_width), lambda i, tab: (tab[z, i], tab[nz + z, i], 0, 0)
        )

    step = lambda w: pl.BlockSpec((1, rows, w), lambda i, tab: (i, 0, 0))
    whole = lambda a: pl.BlockSpec(a.shape, lambda i, tab: (0, 0), pipeline_mode=pl.Buffered(1))
    return pl.pallas_call(
        functools.partial(down_kernel, nz, th, width),
        grid_spec=pltpu.PrefetchScalarGridSpec(
            num_scalar_prefetch=1,
            grid=(count,),
            in_specs=[spec(z) for z in range(nz)]
            + [whole(a) for a in down],
            out_specs=[step(width), step(hid), step(LANES)],
            scratch_shapes=[pltpu.VMEM((hid, width), BF16)],
        ),
        out_shape=[
            jax.ShapeDtypeStruct((count, rows, width), BF16),
            jax.ShapeDtypeStruct((count, rows, hid), F32),
            jax.ShapeDtypeStruct((count, rows, LANES), BF16),
        ],
        compiler_params=pltpu.CompilerParams(vmem_limit_bytes=48 * MEGA),
        cost_estimate=pl.CostEstimate(
            flops=2 * count * rows * hid * width,
            bytes_accessed=count * rows * (4 * width + 4 * hid) + 2 * hid * width,
            transcendentals=0,
        ),
        name="down_rows",
    )(table, *([gathered] * nz), *down)


def chain_kernel(arrays, th, nz, routed, tile, tab, *refs):
    ins = refs[:arrays]
    prod_ref, mask_ref, gate_a, gate_b, up_a, up_b, router_ref = refs[arrays : arrays + 7]
    outs = refs[arrays + 7 : 2 * arrays + 7]
    rows_ref, pg_ref, pu_ref, gh_ref, held, gate_ref, up_ref = refs[2 * arrays + 7 :]
    fill_weights([(gate_a, gate_b, gate_ref), (up_a, up_b, up_ref)])
    i = pl.program_id(0)
    for k in range(arrays):

        @pl.when(tab[arrays, i] == k)
        def _(k=k):
            for z in range(nz):
                rows_ref[0, z * th : (z + 1) * th, :] = ins[k][0, z]

    x = rows_ref[0]
    width = x.shape[1]
    hid = gate_ref.shape[0]
    own = tab[arrays + 1, 0]
    scores = jax.nn.sigmoid(jnp.dot(x, router_ref[...], preferred_element_type=F32))
    chosen = scores * mask_ref[0].astype(F32)
    lane = lax.broadcasted_iota(jnp.int32, chosen.shape, 1)
    mine = jnp.sum(jnp.where(lane == own, chosen, 0.0), axis=1, keepdims=True)
    gate = ROUTE_SCALE * mine / jnp.sum(chosen, axis=1, keepdims=True)
    on = jnp.sum(
        jnp.where(lane == own, mask_ref[0].astype(F32), 0.0), axis=1, keepdims=True
    )
    gate_grad = None
    for j in range(0, hid, tile):
        sl = slice(j, j + tile)
        pre_gate = dot_nt(x, gate_ref[sl, :])
        pre_up = dot_nt(x, up_ref[sl, :])
        prod = prod_ref[0, :, sl]
        sig = jax.nn.sigmoid(pre_gate)
        act = pre_gate * sig
        hidden = act * pre_up
        scale = gate
        part = hidden * prod
        if j + tile > routed:
            column = j + lax.broadcasted_iota(jnp.int32, part.shape, 1)
            scale = jnp.where(column < routed, gate, 1.0)
            part = jnp.where(column < routed, part, 0.0)
        part = jnp.sum(part, axis=1, keepdims=True)
        gate_grad = part if gate_grad is None else gate_grad + part
        upstream = prod * scale
        pg_ref[0, :, sl] = (upstream * pre_up * (sig + act * (1.0 - sig))).astype(BF16)
        pu_ref[0, :, sl] = (upstream * act).astype(BF16)
        gh_ref[0, :, sl] = (hidden * scale).astype(BF16)
    grad = jnp.dot(pg_ref[0], gate_ref[...], preferred_element_type=F32) + jnp.dot(
        pu_ref[0], up_ref[...], preferred_element_type=F32
    )
    held[:, :width] = grad.astype(BF16)
    held[:, width:] = jnp.where(lane == own, gate_grad * on, 0.0).astype(BF16)
    for k in range(arrays):

        @pl.when(tab[arrays, i] == k)
        def _(k=k):
            for z in range(nz):
                outs[k][0, z] = held[z * th : (z + 1) * th, :]


def chain_call(bufs, first, prod, mask, gate, up, router_pad, own, routed, tie):
    arrays = len(bufs)
    steps = [(k, a) for k, buf in enumerate(bufs) for a in range(buf.shape[0])]
    count = len(steps)
    nz, th, width = bufs[0].shape[1:]
    rows = nz * th
    hid = padded(*gate)
    table = np.zeros((arrays + 1, count), np.int32)
    for j in range(arrays):
        table[j] = fill_back([a if k == j else None for k, a in steps])
    table[arrays] = [k for k, _ in steps]
    tab = jnp.concatenate(
        [jnp.asarray(table), jnp.full((1, count), 1, jnp.int32) * own.astype(jnp.int32)], axis=0
    )
    tab = after(tab, tie)
    wide = width + LANES

    def block(j, w):
        return pl.BlockSpec((1, nz, th, w), lambda i, tab: (tab[j, i], 0, 0, 0))

    step = lambda w, base=0: pl.BlockSpec((1, rows, w), lambda i, tab: (i + base, 0, 0))
    whole = lambda a: pl.BlockSpec(a.shape, lambda i, tab: (0, 0), pipeline_mode=pl.Buffered(1))
    return pl.pallas_call(
        functools.partial(chain_kernel, arrays, th, nz, routed, 256),
        grid_spec=pltpu.PrefetchScalarGridSpec(
            num_scalar_prefetch=1,
            grid=(count,),
            in_specs=[block(j, width) for j in range(arrays)]
            + [step(hid, first), step(LANES, first)]
            + [whole(a) for a in (*gate, *up, router_pad)],
            out_specs=[block(j, wide) for j in range(arrays)]
            + [step(width), step(hid), step(hid), step(hid)],
            scratch_shapes=[pltpu.VMEM((rows, wide), BF16)]
            + [pltpu.VMEM((hid, width), BF16)] * 2,
        ),
        out_shape=[jax.ShapeDtypeStruct((*buf.shape[:3], wide), BF16) for buf in bufs]
        + [jax.ShapeDtypeStruct((count, rows, width), BF16)]
        + [jax.ShapeDtypeStruct((count, rows, hid), BF16)] * 3,
        compiler_params=pltpu.CompilerParams(vmem_limit_bytes=56 * MEGA),
        cost_estimate=pl.CostEstimate(
            flops=8 * count * rows * hid * width,
            bytes_accessed=count * rows * (6 * width + 10 * hid) + 4 * hid * width,
            transcendentals=count * rows * hid,
        ),
        name="expert_chain",
    )(tab, *bufs, prod, mask, *gate, *up, router_pad)


def out_kernel(arrays, th, nz, tab, gh_ref, main_ref, extra_ref, *refs):
    outs, held, down_ref = refs[:arrays], refs[arrays], refs[arrays + 1]
    fill_weights([(main_ref, extra_ref, down_ref)])
    i = pl.program_id(0)
    held[...] = jnp.dot(gh_ref[0], down_ref[...], preferred_element_type=F32).astype(BF16)
    for k in range(arrays):

        @pl.when(tab[arrays, i] == k)
        def _(k=k):
            for z in range(nz):
                outs[k][0, z] = held[z * th : (z + 1) * th, :]


def out_call(gated, down, shapes, tie):
    arrays = len(shapes)
    steps = [(k, a) for k, shape in enumerate(shapes) for a in range(shape[0])]
    count = len(steps)
    _, nz, th, width = shapes[0]
    rows = nz * th
    hid = padded(*down)
    table = np.zeros((arrays + 1, count), np.int32)
    for j in range(arrays):
        table[j] = fill_back([a if k == j else None for k, a in steps])
    table[arrays] = [k for k, _ in steps]

    def block(j):
        return pl.BlockSpec((1, nz, th, width), lambda i, tab: (tab[j, i], 0, 0, 0))

    return pl.pallas_call(
        functools.partial(out_kernel, arrays, th, nz),
        grid_spec=pltpu.PrefetchScalarGridSpec(
            num_scalar_prefetch=1,
            grid=(count,),
            in_specs=[
                pl.BlockSpec((1, rows, hid), lambda i, tab: (i, 0, 0)),
            ]
            + [
                pl.BlockSpec(a.shape, lambda i, tab: (0, 0), pipeline_mode=pl.Buffered(1))
                for a in down
            ],
            out_specs=[block(j) for j in range(arrays)],
            scratch_shapes=[pltpu.VMEM((rows, width), BF16), pltpu.VMEM((hid, width), BF16)],
        ),
        out_shape=[jax.ShapeDtypeStruct(shape, BF16) for shape in shapes],
        compiler_params=pltpu.CompilerParams(vmem_limit_bytes=48 * MEGA),
        cost_estimate=pl.CostEstimate(
            flops=2 * count * rows * hid * width,
            bytes_accessed=count * rows * 2 * (width + hid) + 2 * hid * width,
            transcendentals=0,
        ),
        name="expert_out",
    )(after(jnp.asarray(table), tie), gated, *down)


def weight_kernel(calls, per, outs_n, hid, extra, tie_ref, *refs):
    lefts, rights = refs[: calls * outs_n], refs[calls * outs_n : calls * (outs_n + 1)]
    outs = refs[calls * (outs_n + 1) :]
    i = pl.program_id(0)

    @pl.when(i == 0)
    def _():
        for o in outs:
            o[...] = jnp.zeros_like(o)

    for c in range(calls):

        @pl.when(i // per == c)
        def _(c=c):
            right = rights[c][0]
            for k in range(outs_n):
                full = lax.dot_general(
                    lefts[k * calls + c][0],
                    right,
                    (((0,), (0,)), ((), ())),
                    preferred_element_type=F32,
                )
                outs[k][...] += full[:hid]
                outs[outs_n + k][...] += full[hid : hid + extra]


def weight_call(lefts, rights, hid, extra, tie):
    calls, outs_n = len(rights), len(lefts)
    bases = [r[1] if len(r) > 1 else 0 for r in rights]
    rights = [r[0] for r in rights]
    per, rows, pad = lefts[0][0].shape
    width = rights[0].shape[2]
    if per % 2 == 0 and rows <= 256:
        rights = [r.reshape(r.shape[0] // 2, 2 * rows, width) for r in rights]
        lefts = [[a.reshape(per // 2, 2 * rows, pad) for a in left] for left in lefts]
        per, rows, bases = per // 2, 2 * rows, [base // 2 for base in bases]

    def spec(c, w, base=0):
        return pl.BlockSpec(
            (1, rows, w), lambda i: (base + jnp.clip(i - c * per, 0, per - 1), 0, 0)
        )

    return pl.pallas_call(
        functools.partial(weight_kernel, calls, per, outs_n, hid, extra),
        grid=(calls * per,),
        in_specs=[pl.BlockSpec(memory_space=pl.ANY)]
        + [spec(c, pad) for _ in range(outs_n) for c in range(calls)]
        + [spec(c, width, bases[c]) for c in range(calls)],
        out_specs=[pl.BlockSpec((hid, width), lambda i: (0, 0))] * outs_n
        + [pl.BlockSpec((extra, width), lambda i: (0, 0))] * outs_n,
        out_shape=[jax.ShapeDtypeStruct((hid, width), F32)] * outs_n
        + [jax.ShapeDtypeStruct((extra, width), F32)] * outs_n,
        compiler_params=pltpu.CompilerParams(vmem_limit_bytes=58 * MEGA),
        cost_estimate=pl.CostEstimate(
            flops=2 * outs_n * calls * per * rows * pad * width,
            bytes_accessed=calls * per * rows * 2 * (outs_n * pad + width) + 4 * outs_n * hid * width,
            transcendentals=0,
        ),
        name="expert_weights",
    )(after(jnp.zeros((8, LANES), F32), tie), *[a for left in lefts for a in left], *rights)


def rotary_tables(segment_row):
    length = segment_row.shape[-1]
    places = jnp.arange(length, dtype=jnp.int32)
    same_document = segment_row[:, :, None] == segment_row[:, None, :]
    position = jnp.sum(
        jnp.where(same_document & (places[None, :] < places[:, None])[None], 1.0, 0.0), axis=2
    )
    half_rope = ROPE // 2
    frequency = ROTARY_BASE ** (-2.0 * jnp.arange(half_rope, dtype=F32) / ROPE)
    angles = position[:, :, None] * frequency
    cosine = jnp.concatenate([jnp.cos(angles), jnp.cos(angles)], axis=-1)
    sine_table = jnp.concatenate([jnp.sin(angles), jnp.sin(angles)], axis=-1)
    allowed = same_document & (places[None, :] <= places[:, None])[None]
    return cosine, sine_table, allowed


def rotate(values, cosine, sine_table):
    half_rope = values.shape[-1] // 2
    turned = jnp.concatenate([-values[..., half_rope:], values[..., :half_rope]], axis=-1)
    return values * cosine + turned * sine_table


def unrotate(upstream, cosine, sine_table):
    half_rope = upstream.shape[-1] // 2
    weighted = upstream * sine_table
    turned = jnp.concatenate([weighted[..., half_rope:], -weighted[..., :half_rope]], axis=-1)
    return upstream * cosine + turned


def einsum(pattern, a, b):
    return jnp.einsum(pattern, a, b, preferred_element_type=F32)


def body(
    tokens,
    segment_ids,
    routes,
    attn_gain,
    w_query,
    w_latent,
    latent_gain,
    w_keyval,
    w_output,
    ffn_gain,
    w_router,
    shared_gate,
    shared_up,
    shared_down,
    expert_gate,
    expert_up,
    expert_down,
    cotangent,
):
    net = Net()
    S, E, s, e = net.S, net.E, net.s, net.e
    T, D = tokens.shape
    DK = D // S
    HL = HEADS // S
    HQ = HL * (NOPE + ROPE)
    HV = HL * (NOPE + VDIM)
    HID = shared_down.shape[0]
    blocks = list(range(S))

    def cols(value, index, size):
        return lax.dynamic_slice_in_dim(value, (index % S) * size, size, value.ndim - 1)

    def pair_rows(value):
        return jnp.stack(net.ring_gather(value, "y"), axis=0)

    def pair_sum_blocks(parts):
        total = parts[0].astype(F32)
        for r in range(1, S):
            total = total + net.hop(parts[r].astype(BF16), "y", r).astype(F32)
        return total

    KR = KVR // S
    packed = jnp.concatenate(
        [
            w_router.T,
            ffn_gain[None],
            jnp.pad(latent_gain, (0, DK - KR))[None],
        ],
        axis=0,
    )
    packed = net.ring_gather(packed, "y")
    router_full = net.absolute([p[:E] for p in packed], "y", 1)
    ffn_gain_full = net.absolute([p[E] for p in packed], "y", 0).astype(F32)
    latent_gain_full = net.absolute([p[E + 1, :KR] for p in packed], "y", 0).astype(F32)
    inputs = tokens.astype(F32)
    scale_one = norm_scale(inputs)
    rows2 = jnp.concatenate([segment_ids.astype(F32), scale_one.reshape(1, T)], axis=0)
    rows2 = jnp.stack(net.ring_gather(rows2, "y"), axis=0)
    seg_pair = rows2[:, 0]
    scales = rows2[:, 1].reshape(S, T, 1)
    x_pieces = [cols(tokens, s, DK)] + [None] * (S - 1)
    for r in range(1, S):
        x_pieces[S - r] = net.hop(cols(tokens, s + r, DK), "y", r)
    x_cols = jnp.stack(x_pieces, axis=0).astype(F32)
    attn_gain_f = attn_gain.astype(F32)
    plain_one = x_cols * scales
    normed_one = (plain_one * attn_gain_f).astype(BF16).reshape(S * T, DK)
    cosine, sine_table, allowed = rotary_tables(seg_pair)

    query_parts = [
        dot(normed_one, cols(w_query, s + r, HQ)).astype(BF16).reshape(S, T, HQ)
        for r in range(1, S)
    ]
    latent_part_own = dot(normed_one, w_latent).reshape(S, T, -1)
    latent_sent = latent_part_own.astype(BF16)
    query_got = [net.hop(part, "y", r) for r, part in enumerate(query_parts, 1)]
    latent_got = [net.hop(latent_sent, "y", r) for r in range(1, S)]
    first = query_got
    core = net.pos("c")
    half_rows = KR // net.n["c"]
    kv_half = lax.dynamic_slice_in_dim(w_keyval, core * half_rows, half_rows, 0)
    kv_pieces = [cols(w_keyval, s, HV)] + [None] * (S - 1)
    for r in range(1, S):
        got = net.hop(after(cols(kv_half, s + r, HV), first), "y", r)
        kv_pieces[S - r] = net.absolute(net.ring_gather(got, "c"), "c", 0)
    keyval_full = net.absolute(kv_pieces, "y", 0)

    HS = HID // E
    HP = -(-HS // 16) * 16
    sh_pieces = [None] * S
    for r in range(S):
        mine = [
            lax.dynamic_slice_in_dim(w, ((s + r) % S) * HID + e * HS, HS, 1).T
            for w in (shared_gate, shared_up)
        ]
        mine = jnp.pad(jnp.stack(mine, axis=0), ((0, 0), (0, HP - HS), (0, 0)))
        mine = after(mine, first)
        sh_pieces[(S - r) % S] = net.hop(mine, "y", r) if r else mine
    sh_slices = net.absolute(sh_pieces, "y", 2)
    sh_down = lax.dynamic_slice_in_dim(shared_down, e * HS, HS, 0)
    sh_down = after(jnp.pad(sh_down, ((0, HP - HS), (0, 0))), first)
    down_t = (expert_down[0], sh_down)
    gate_t = (expert_gate[0].T, sh_slices[0])
    up_t = (expert_up[0].T, sh_slices[1])
    router_pad = jnp.pad(router_full.T, ((0, 0), (0, LANES - E)))

    queries = dot(normed_one, cols(w_query, s, HQ)).reshape(S, T, HQ)
    for r, got in enumerate(query_got, 1):
        queries = queries + jnp.concatenate([got[r:], got[:r]], axis=0).astype(F32)
    queries = queries.reshape(S, T, HL, NOPE + ROPE)

    def block_all_sum(value):
        total = value
        for r in range(1, S):
            got = net.hop(value.astype(BF16), "y", r).astype(F32)
            total = total + jnp.concatenate([got[r:], got[:r]], axis=0)
        return total

    latent_all = latent_part_own
    for r, got in enumerate(latent_got, 1):
        latent_all = latent_all + jnp.concatenate([got[r:], got[:r]], axis=0).astype(F32)
    query_turn = rotate(queries[..., NOPE:], cosine[:, :, None, :], sine_table[:, :, None, :])
    query_b = jnp.concatenate([queries[..., :NOPE], query_turn], axis=-1).astype(BF16)
    latent = latent_all[..., :KVR]
    key_rope = rotate(latent_all[..., KVR:], cosine, sine_table)
    scale_latent = norm_scale(latent)
    latent_normed = (latent * scale_latent * latent_gain_full).astype(BF16)
    keyval = dot(latent_normed.reshape(S * T, KVR), keyval_full).reshape(S, T, HL, NOPE + VDIM)
    key_shared = jnp.broadcast_to(key_rope[:, :, None, :], (S, T, HL, ROPE))
    key_b = jnp.concatenate([keyval[..., :NOPE], key_shared], axis=-1).astype(BF16)
    value_b = keyval[..., NOPE:].astype(BF16)
    att_scale = (NOPE + ROPE) ** (-0.5)
    scores = einsum("bthd,bshd->bhts", query_b, key_b) * att_scale
    scores = jnp.where(allowed[:, None], scores, NEGATIVE)
    peak = jnp.max(scores, axis=-1, keepdims=True)
    raised = jnp.exp(scores - peak)
    probs = raised / jnp.sum(raised, axis=-1, keepdims=True)
    probs_b = probs.astype(BF16)
    attended = einsum("bhts,bshd->bthd", probs_b, value_b)
    attended = after(attended, sh_slices).astype(BF16).reshape(S * T, HL * VDIM)
    out_parts = dot(attended, w_output).reshape(S, T, D)
    residual = inputs + pair_sum_blocks([out_parts[r] for r in blocks])
    scale_two = norm_scale(residual)
    normed_two = (residual * scale_two * ffn_gain_full).astype(BF16)

    th = T // 2
    nx, ny, nz, nc = net.n["x"], net.n["y"], net.n["z"], net.n["c"]
    ids = jnp.arange(E, dtype=jnp.int32)
    mask_own = jnp.sum((routes[:, :, None] == ids[None, None, :]).astype(F32), axis=1)
    mask_lanes = jnp.pad(mask_own.astype(BF16), ((0, 0), (0, LANES - E)))
    cot_wide = jnp.concatenate([cotangent, mask_lanes], axis=1)
    cot_gathered = lax.all_gather(cot_wide, ("expert", "shard"), axis=0).reshape(
        E * S, 2, th, D + LANES
    )
    nr = max(nx, ny)
    steps = []
    for r in range(nr):
        for p in range(2):
            for c in range(nc):
                for k in range(nx if p == 0 else ny):
                    steps.append((k, c, r, p) if p == 0 else (r, c, k, p))
    at = {axis: net.pos(axis) for axis in "cxzy"}
    ahead = lambda axis, k: (at[axis] + jnp.asarray(k, jnp.int32)) % net.n[axis]
    step_x, step_c, step_y, step_p = [np.array(v, np.int32) for v in zip(*steps)]
    table = []
    for z in range(nz):
        expert_of = (
            ahead("z", z) * net.stride["z"]
            + ahead("x", step_x) * net.stride["x"]
            + ahead("c", step_c) * net.stride["c"]
        )
        table.append(expert_of * S + ahead("y", step_y))
    table = jnp.stack(table + [jnp.asarray(step_p)] * nz, axis=0).astype(jnp.int32)
    cot_rows, cot_prod, mask_rows = down_call(cot_gathered, table, down_t, th, D)
    tok_1 = net.gather_part(normed_two[:th], "x", mask_rows)
    tok_2 = net.gather_part(normed_two[th:], "y", mask_rows)
    per = len(steps) // nr
    in_1, in_2 = [], []
    x_rows, pg_rows, pu_rows, gh_rows = [], [], [], []
    for r in range(nr):
        if r == 0:
            bufs, tie = tok_1[0] + tok_2[0], ()
        else:
            tie = gh_rows[-1]
            far = after((tok_1[1][r - 1], tok_2[1][r - 1]), tie)
            bufs = net.ring_gather(far[0], "c") + net.ring_gather(far[1], "c")
        got = chain_call(
            bufs, r * per, cot_prod, mask_rows, gate_t, up_t, router_pad, e, HID, tie
        )
        in_1.append(got[:nc])
        in_2.append(got[nc : 2 * nc])
        x_rows.append(got[2 * nc])
        pg_rows.append(got[2 * nc + 1])
        pu_rows.append(got[2 * nc + 2])
        gh_rows.append(got[2 * nc + 3])
    in_sum_1, in_sum_2 = net.scatter_cores(in_1), net.scatter_cores(in_2)
    shapes = [buf.shape for buf in tok_1[0] + tok_2[0]]
    weight_grads, out_sums, out_bufs = {}, [], []

    def weights_of(name, rows, rights, tie):
        weight_grads[name] = weight_call([rows], rights, HID, HS, tie)
        return weight_grads[name]

    def gate_up_work(marks):
        rights = [[v] for v in x_rows]
        one = weights_of("gate", pg_rows, rights, marks)
        return [weights_of("up", pu_rows, rights, one[1])[1]]

    def down_work(marks):
        rights = [(cot_rows, r * per) for r in range(nr)]
        return weights_of("down", gh_rows, rights, marks)[1]

    def out_work(r):
        def job(marks):
            out_bufs.append(out_call(gh_rows[r], down_t, shapes, marks))
            return out_bufs[-1][0]

        return job

    def out_sum_work(marks):
        for bufs in out_bufs:
            out_sums.append([net.ring_list(bufs[:nc], "c"), net.ring_list(bufs[nc:], "c")])
        return [v[0] for v in out_sums]

    hops = max(nx, ny) - 1
    work = [gate_up_work] + [None] * (hops - 1) + [down_work] + [None] * (hops - 1)
    early = min(nr, nz - 2)
    work += [out_work(r) for r in range(early)]
    if early == nr:
        work.append(out_sum_work)
    in_wide = net.scatter_both(in_sum_1, in_sum_2, work)
    gate_w_grad, sh_gate_rows = weight_grads["gate"]
    up_w_grad, sh_up_rows = weight_grads["up"]
    down_grad, sh_down_rows = weight_grads["down"]
    in_grad = in_wide[:, :D]
    gate_grads_raw = in_wide[:, D : D + E].astype(F32)

    def gather_cols(value, width):
        pieces = [value.reshape(S, T, width)] + [None] * (S - 1)
        for r in range(1, S):
            got = net.hop(value.reshape(S, T, width), "y", r)
            pieces[S - r] = jnp.concatenate([got[r:], got[:r]], axis=0)
        return net.absolute(pieces, "y", 2).reshape(S * T, S * width)

    def own_cols(value):
        pieces = [value[0].astype(BF16)] + [None] * (S - 1)
        for r in range(1, S):
            pieces[S - r] = net.hop(value[r].astype(BF16), "y", r)
        return net.absolute(pieces, "y", 1).astype(F32)

    scores_own = jax.nn.sigmoid(dot_tr(normed_two, router_full))
    gate_grads = gate_grads_raw * mask_own
    picked = scores_own * mask_own
    picked_total = jnp.sum(picked, axis=1, keepdims=True)
    weighted = jnp.sum(gate_grads * picked, axis=1, keepdims=True)
    picked_grad = ROUTE_SCALE * (
        gate_grads / picked_total - weighted / (picked_total * picked_total)
    )
    logit_grad_b = (picked_grad * picked * (1.0 - picked)).astype(BF16)
    normed_two_grad = in_grad.astype(F32) + dot(logit_grad_b, router_full)
    upstream = cotangent.astype(F32)
    plain_two = residual * scale_two
    ffn_gain_part = jnp.sum(normed_two_grad * plain_two, axis=0)
    inner = normed_two_grad * ffn_gain_full
    residual_grad = upstream + scale_two * (
        inner - plain_two * jnp.mean(inner * plain_two, axis=-1, keepdims=True)
    )
    router_grad_part = dot_tl(normed_two, logit_grad_b)

    room = ((0, HP - HS), (0, 0))
    sh_gu = jnp.stack([jnp.pad(v.astype(BF16), room) for v in (sh_gate_rows, sh_up_rows)], axis=0)
    sh_down_own = jnp.pad(sh_down_rows.astype(BF16), room)
    gu_pieces = [None] * S
    for r in range(S):
        piece = cols(sh_gu, s + r, DK)
        gu_pieces[(S - r) % S] = net.hop(piece, "y", r) if r else piece
    gu_own = net.absolute([piece[:, None] for piece in gu_pieces], "y", 1).reshape(2 * S * HP, DK)
    gu_all = lax.all_gather(gu_own, "expert", axis=0, tiled=True)
    down_all = lax.all_gather(sh_down_own, "expert", axis=0, tiled=True)

    grad_b = net.ring_gather(residual_grad.astype(BF16), "y")
    grad_b = jnp.stack(grad_b, axis=0).reshape(S * T, D)
    output_part = dot_tl(attended, grad_b)
    attended_grad = dot_tr(grad_b, w_output).astype(BF16).reshape(S, T, HL, VDIM)
    value_grad = einsum("bhts,bthd->bshd", probs_b, attended_grad)
    probs_grad = einsum("bthd,bshd->bhts", attended_grad, value_b)
    center = jnp.sum(probs * probs_grad, axis=-1, keepdims=True)
    output_part = after(output_part, gu_all, down_all).astype(BF16)
    output_w = lax.psum(output_part, "expert")
    scores_grad = (after(probs, output_part) * (probs_grad - center) * att_scale).astype(BF16)
    query_grad = einsum("bhts,bshd->bthd", scores_grad, key_b)
    key_grad = einsum("bhts,bthd->bshd", scores_grad, query_b)
    query_turn_grad = unrotate(
        query_grad[..., NOPE:], cosine[:, :, None, :], sine_table[:, :, None, :]
    )
    query_grad_b = (
        jnp.concatenate([query_grad[..., :NOPE], query_turn_grad], axis=-1)
        .astype(BF16)
        .reshape(S * T, HQ)
    )
    query_grad_all = gather_cols(query_grad_b, HQ)
    if not out_sums:
        for r in range(early, nr):
            out_work(r)(query_grad_b)
        out_sum_work(())
    keyval_grad_b = (
        jnp.concatenate([key_grad[..., :NOPE], value_grad], axis=-1)
        .astype(BF16)
        .reshape(S * T, HV)
    )
    latent_part = dot_tr(keyval_grad_b, keyval_full).reshape(S, T, KVR)
    rope_part = jnp.sum(key_grad[..., NOPE:], axis=2)
    latent_sum = block_all_sum(jnp.concatenate([latent_part, rope_part], axis=-1))
    latent_up = latent_sum[..., :KVR]
    key_rope_grad = unrotate(latent_sum[..., KVR:], cosine, sine_table)
    plain_latent = latent * scale_latent
    latent_gain_part = jnp.sum(latent_up * plain_latent, axis=(0, 1))
    inner_latent = latent_up * latent_gain_full
    latent_grad = scale_latent * (
        inner_latent - plain_latent * jnp.mean(inner_latent * plain_latent, axis=-1, keepdims=True)
    )
    latent_all_grad = (
        jnp.concatenate([latent_grad, key_rope_grad], axis=-1).astype(BF16).reshape(S * T, -1)
    )
    normed_grad = dot_tr(query_grad_all, w_query) + dot_tr(latent_all_grad, w_latent)
    plain_flat = plain_one.reshape(S * T, DK)
    attn_gain_part = jnp.sum(normed_grad * plain_flat, axis=0)
    inner_one = own_cols((normed_grad * attn_gain_f).reshape(S, T, DK))
    plain_own = inputs * scale_one
    tokens_grad = residual_grad + scale_one * (
        inner_one - plain_own * jnp.mean(inner_one * plain_own, axis=-1, keepdims=True)
    )

    query_part = dot_tl(normed_one, query_grad_all).astype(BF16)
    ffn_part, router_part = after((ffn_gain_part, router_grad_part), query_part)
    small_ffn = cols(ffn_part, s, DK)
    small_router = cols(router_part.T, s, DK)
    for r in range(1, S):
        sent = jnp.concatenate(
            [cols(ffn_part, s + r, DK)[None], cols(router_part.T, s + r, DK)], axis=0
        )
        got = net.hop(sent, "y", r)
        small_ffn = small_ffn + got[0]
        small_router = small_router + got[1:]
    latent_rows = dot_tl(latent_all_grad, normed_one).astype(BF16)
    small = jnp.concatenate(
        [
            attn_gain_part[None],
            small_ffn[None],
            jnp.pad(cols(latent_gain_part, s, KR), (0, DK - KR))[None],
            small_router,
        ],
        axis=0,
    )
    LW = latent_rows.shape[0]
    xz = ("c", "x", "z")
    output_w = output_w.astype(F32)
    tot_q, tot_l = lax.psum((query_part, latent_rows), "expert")
    tot_s = small
    for axis in "cxz":
        pieces = net.ring_gather(tot_s, axis)
        tot_s = functools.reduce(jnp.add, pieces)

    row_ids = after(jnp.arange(E * 2 * S * HP, dtype=jnp.int32), query_part)
    at_hidden = (
        ((row_ids // (HP * S)) % 2) * (S * HID)
        + ((row_ids // HP) % S) * HID
        + (row_ids // (HP * S * 2)) * HS
        + row_ids % HP
    )
    at_hidden = jnp.where(row_ids % HP < HS, at_hidden, -1)
    hidden_ids = jnp.arange(S * HID, dtype=jnp.int32)
    shared_gate_w = dot_tl(gu_all, (at_hidden[:, None] == hidden_ids[None]).astype(BF16))
    shared_up_w = dot_tl(gu_all, (at_hidden[:, None] == S * HID + hidden_ids[None]).astype(BF16))
    row_ids = after(jnp.arange(E * HP, dtype=jnp.int32), query_part)
    at_hidden = jnp.where(row_ids % HP < HS, (row_ids // HP) * HS + row_ids % HP, -1)
    place_down = (jnp.arange(HID, dtype=jnp.int32)[:, None] == at_hidden[None]).astype(BF16)
    shared_down_w = dot(place_down, down_all)

    def keyval_steps():
        piece = dot_tl(keyval_grad_b, latent_normed.reshape(S * T, KVR))
        piece = after(piece, query_part).astype(BF16)
        piece = yield from net.reduce_steps(piece, xz)
        mine = [cols(piece, s, KR)] + [None] * (S - 1)
        for r in range(1, S):
            mine[S - r] = net.hop(cols(piece, s + r, KR), "y", r)
        mine = net.absolute([p[None] for p in mine], "y", 0)
        value = yield from net.spread_steps(mine, xz, dim=1)
        return value

    out_1, out_2 = [v[0] for v in out_sums], [v[1] for v in out_sums]
    split = lambda v: [v[k] for k in range(v.shape[0])]
    got = net.scatter_stage(
        [split(v) for v in out_1] + [out_2],
        ("x",) * (len(out_1) + 1),
        [lambda marks: query_part] + [None] * (nx - 2),
    )
    one, two = net.scatter_stage([got[:-1], split(got[-1])], ("y", "y"))
    one = [jnp.concatenate([one[k], two[k]], axis=0) for k in range(nz)]
    routed = net.scatter_stage([one], ("z",))[0].astype(F32)
    (kv_all,) = net.in_rounds([keyval_steps()])
    block_out = (residual + routed).astype(BF16)
    keyval_w = dot_tr(jnp.eye(KR, dtype=BF16), kv_all.reshape(S * HV, KR))
    query_w = tot_q.astype(F32)
    latent_w = tot_l.astype(F32).T
    return (
        block_out,
        tokens_grad,
        tot_s[0],
        query_w,
        latent_w,
        tot_s[2, :KR],
        keyval_w,
        output_w,
        tot_s[1],
        tot_s[3:].T,
        shared_gate_w,
        shared_up_w,
        shared_down_w,
        gate_w_grad.T[None],
        up_w_grad.T[None],
        down_grad[None],
    )


def solution(mesh):
    both = P(("expert", "shard"), None)
    row = P("shard", None)
    in_specs = (
        both, both, both, P("shard"), row, row, P("shard"), row, row, P("shard"), row, row, row, row,
        P("expert", None, "shard"), P("expert", None, "shard"), P("expert", "shard", None), both,
    )
    out_specs = (
        both, both, P("shard"), row, row, P("shard"), row, row, P("shard"), row, row, row, row,
        P("expert", None, "shard"), P("expert", None, "shard"), P("expert", "shard", None),
    )
    return jax.shard_map(body, mesh=mesh, in_specs=in_specs, out_specs=out_specs, check_vma=False)
```
